32 devices in a mesh: replica: 4 (over y, x), shard: 8 (over z, core).
Axes of the slice: x: 2, y: 2, z: 4, core: 2. Of those that a mesh axis runs over, the one named last changes fastest.
Arguments:
- hidden: bfloat16 [4, 1024, 1024], P('replica', 'shard'), may hold values from -6 to 6
- encoded: bfloat16 [4, 1024, 1024], P('replica', 'shard'), may hold values from -6 to 6
- cotangent: bfloat16 [4, 1024, 1024], P('replica', 'shard'), may hold values from -6 to 6
- norm_gain: bfloat16 [1024, 3], P('shard'), may hold values from 0.5 to 1.5
- norm_bias: bfloat16 [1024, 3], P('shard'), may hold values from -2 to 2
- attn_bias: bfloat16 [1024, 4], P('shard'), may hold values from -3 to 3
- out_bias: bfloat16 [1024, 3], P('shard'), may hold values from -2 to 2
- self_qkv: bfloat16 [1024, 3072], P('shard'), may hold values from -0.1875 to 0.1875
- self_out: bfloat16 [1024, 1024], P('shard'), may hold values from -3 to 3
- cross_q: bfloat16 [1024, 1024], P('shard'), may hold values from -0.1875 to 0.1875
- cross_kv: bfloat16 [1024, 2048], P('shard'), may hold values from -0.1875 to 0.1875
- cross_out: bfloat16 [1024, 1024], P('shard'), may hold values from -3 to 3
- ffn_in: bfloat16 [1024, 4096], P('shard'), may hold values from -0.1875 to 0.1875
- ffn_in_bias: bfloat16 [4096], P('shard'), may hold values from -3 to 3
- ffn_out: bfloat16 [4096, 1024], P('shard'), may hold values from -0.09375 to 0.09375
Outputs:
- output: bfloat16 [4, 1024, 1024], P('replica', 'shard')
- hidden_grad: float32 [4, 1024, 1024], P('replica', 'shard')
- encoded_grad: float32 [4, 1024, 1024], P('replica', 'shard')
- norm_gain_grad: float32 [1024, 3], P('shard')
- norm_bias_grad: float32 [1024, 3], P('shard')
- attn_bias_grad: float32 [1024, 4], P('shard')
- out_bias_grad: float32 [1024, 3], P('shard')
- self_qkv_grad: float32 [1024, 3072], P('shard')
- self_out_grad: float32 [1024, 1024], P('shard')
- cross_q_grad: float32 [1024, 1024], P('shard')
- cross_kv_grad: float32 [1024, 2048], P('shard')
- cross_out_grad: float32 [1024, 1024], P('shard')
- ffn_in_grad: float32 [1024, 4096], P('shard')
- ffn_in_bias_grad: float32 [4096], P('shard')
- ffn_out_grad: float32 [4096, 1024], P('shard')
The draws below stay inside these ranges and needn't reach their ends.
All inputs are finite; a program needn't handle non-finite values.
Results may differ from the reference program's by a relative error of at most 0.025.
Values may be sent and summed in bfloat16 or wider, within the bound.
No kernel may reach another device: no remote copies, remote signals or barrier semaphores. Data moves between devices by JAX's collectives and lax.ppermute only.
A program may use at most 256 MiB of HBM per device.

```python
import jax
import jax.numpy as jnp
from jax import lax

D = 1024
HEADS = 16
FF = 4096
HEAD_DIM = 64
LEN = 1024
SEQS = 4


def block_levels(stream_key, dims, cuts, smallest, largest):
    def one(axis_at, shards_of):
        draws = jax.random.uniform(jax.random.fold_in(jax.random.fold_in(stream_key, 6), axis_at), (shards_of,), jnp.float32, smallest / len(cuts), largest / len(cuts))
        return jnp.repeat(jnp.exp(draws), dims[axis_at] // shards_of).reshape((-1,) + (1,) * (len(dims) - axis_at - 1))

    gain = one(*cuts[0])
    for cut in cuts[1:]:
        gain = gain * one(*cut)
    return gain


def noise(key, shape, width, bound, pieces=(), kind=jnp.bfloat16):
    entries = jax.random.normal(key, shape, jnp.float32) * width
    if len(pieces) > 0:
        entries = block_levels(key, shape, pieces, -0.22, 0.18) * entries
    return jnp.clip(entries, min=-bound, max=bound).astype(kind)


def setup_inputs(seed: int = 0) -> dict:
    arg_keys = jax.random.split(jax.random.key(seed), 16)
    hidden = noise(arg_keys[0], (SEQS, LEN, D), 1.0, 6.0, ((0, 4), (1, 8)))
    encoded = noise(arg_keys[1], (SEQS, LEN, D), 1.0, 6.0, ((0, 4), (1, 8)))
    cotangent = noise(arg_keys[2], (SEQS, LEN, D), 1.0, 6.0, ((0, 4), (1, 8)))
    norm_gain = jnp.clip(1.0 + 0.1 * jax.random.normal(arg_keys[3], (D, 3), jnp.float32), 0.5, 1.5).astype(jnp.bfloat16)
    norm_bias = noise(arg_keys[4], (D, 3), 0.3, 2.0, ((0, 8),))
    attn_bias = noise(arg_keys[5], (D, 4), 0.5, 3.0, ((0, 8),))
    out_bias = noise(arg_keys[6], (D, 3), 0.3, 2.0, ((0, 8),))
    self_qkv = noise(arg_keys[7], (D, 3 * D), D ** -0.5, 0.1875, ((0, 8),))
    self_out = noise(arg_keys[8], (D, D), (max(1, 4 * D // LEN)) ** -0.5, 3.0, ((0, 8),))
    cross_q = noise(arg_keys[9], (D, D), D ** -0.5, 0.1875, ((0, 8),))
    cross_kv = noise(arg_keys[10], (D, 2 * D), D ** -0.5, 0.1875, ((0, 8),))
    cross_out = noise(arg_keys[11], (D, D), (max(1, 4 * D // LEN)) ** -0.5, 3.0, ((0, 8),))
    ffn_in = noise(arg_keys[12], (D, FF), D ** -0.5, 0.1875, ((0, 8),))
    ffn_in_bias = noise(arg_keys[13], (FF,), 0.5, 3.0, ((0, 8),))
    ffn_out = noise(arg_keys[14], (FF, D), FF ** -0.5, 0.09375, ((0, 8),))
    return {"hidden": hidden, "encoded": encoded, "cotangent": cotangent, "norm_gain": norm_gain, "norm_bias": norm_bias, "attn_bias": attn_bias, "out_bias": out_bias, "self_qkv": self_qkv, "self_out": self_out, "cross_q": cross_q, "cross_kv": cross_kv, "cross_out": cross_out, "ffn_in": ffn_in, "ffn_in_bias": ffn_in_bias, "ffn_out": ffn_out}


HIGHEST = lax.Precision.HIGHEST

@jax.custom_vjp
def low(v):
    return lax.optimization_barrier(v.astype(jnp.bfloat16)).astype(jnp.float32)

@jax.custom_vjp
def low_back(v):
    return v

def low_keep(v):
    return (low(v), None)

def low_pass(kept, grad):
    return (grad,)

def back_keep(v):
    return (v, None)

def back_low(kept, grad):
    return (low(grad),)
low.defvjp(low_keep, low_pass)
low_back.defvjp(back_keep, back_low)

def product(left_side, right_side):
    return jnp.dot(left_side, right_side, precision=HIGHEST)

def rounded_both(values_in):
    return low_back(low(values_in))

def layer_norm(values_in, norm_scale, norm_shift):
    average = lax.optimization_barrier(jnp.mean(values_in, axis=-1, keepdims=True))
    centred = values_in - average
    variance = lax.optimization_barrier(jnp.mean(centred * centred, axis=-1, keepdims=True))
    return centred * lax.rsqrt(variance + 1e-05) * norm_scale + norm_shift

def attention(queries, keys_all, values_all, causal):
    block_rows = min(512, LEN)
    block_count = LEN // block_rows
    query_heads = queries.reshape(LEN, HEADS, HEAD_DIM)
    key_heads = keys_all.reshape(LEN, HEADS, HEAD_DIM)
    value_heads = values_all.reshape(LEN, HEADS, HEAD_DIM)

    def one_block(block_index):
        start_row = block_index * block_rows
        query_rows = lax.dynamic_slice_in_dim(query_heads, start_row, block_rows, 0)
        scores = jnp.einsum('qhd,khd->hqk', query_rows, key_heads, precision=HIGHEST) * HEAD_DIM ** (-0.5)
        if causal:
            positions = start_row + jnp.arange(block_rows, dtype=jnp.int32)
            allowed = positions[:, None] >= jnp.arange(LEN, dtype=jnp.int32)[None, :]
            scores = jnp.where(allowed[None], scores, -1e+30)
        scores = low_back(scores)
        row_max = lax.optimization_barrier(jnp.max(scores, axis=-1, keepdims=True))
        weights = jnp.exp(scores - row_max)
        probabilities = low(weights / lax.optimization_barrier(jnp.sum(weights, axis=-1, keepdims=True)))
        context = jnp.einsum('hqk,khd->qhd', probabilities, value_heads, precision=HIGHEST)
        return context.reshape(block_rows, D)
    blocks = lax.map(jax.checkpoint(one_block), jnp.arange(block_count, dtype=jnp.int32))
    return blocks.reshape(LEN, D)

def layer(state_rows, memory, params):
    norm_gains, norm_shifts, pair_biases, branch_biases, qkv_weight, self_projection, cross_query_weight, cross_pair_weight, cross_projection, ffn_up, ffn_shift, ffn_down = params
    normed = low(layer_norm(state_rows, norm_gains[:, 0], norm_shifts[:, 0]))
    joined = product(normed, qkv_weight)
    queries = rounded_both(joined[:, :D] + pair_biases[:, 0])
    keys_self = rounded_both(joined[:, D:2 * D])
    values_self = rounded_both(joined[:, 2 * D:] + pair_biases[:, 1])
    context = rounded_both(attention(queries, keys_self, values_self, True))
    first = state_rows + low_back(product(context, self_projection) + branch_biases[:, 0])
    normed = low(layer_norm(first, norm_gains[:, 1], norm_shifts[:, 1]))
    cross_queries = rounded_both(product(normed, cross_query_weight) + pair_biases[:, 2])
    memory_pair = product(memory, cross_pair_weight)
    cross_keys = rounded_both(memory_pair[:, :D])
    cross_values = rounded_both(memory_pair[:, D:] + pair_biases[:, 3])
    context = rounded_both(attention(cross_queries, cross_keys, cross_values, False))
    second = first + low_back(product(context, cross_projection) + branch_biases[:, 1])
    normed = low(layer_norm(second, norm_gains[:, 2], norm_shifts[:, 2]))
    hidden_pre = low_back(product(normed, ffn_up) + ffn_shift)
    activated = low(jax.nn.gelu(hidden_pre, approximate=False))
    return second + low_back(product(activated, ffn_down) + branch_biases[:, 2])

def reference(hidden, encoded, cotangent, norm_gain, norm_bias, attn_bias, out_bias, self_qkv, self_out, cross_q, cross_kv, cross_out, ffn_in, ffn_in_bias, ffn_out):
    params = tuple((weight.astype(jnp.float32) for weight in (norm_gain, norm_bias, attn_bias, out_bias, self_qkv, self_out, cross_q, cross_kv, cross_out, ffn_in, ffn_in_bias, ffn_out)))

    def one_sequence(totals, inputs):
        state_rows, memory, seed_grad = inputs
        result, pullback = jax.vjp(layer, state_rows, memory, params)
        grad_state, grad_memory, grad_params = pullback(seed_grad)
        totals = jax.tree.map(lambda first_term, second_term: first_term + second_term, totals, grad_params)
        return (totals, (result.astype(jnp.bfloat16), grad_state, grad_memory))
    zeros = tuple((jnp.zeros_like(weight) for weight in params))
    totals, outputs = lax.scan(one_sequence, zeros, (hidden.astype(jnp.float32), encoded.astype(jnp.float32), cotangent.astype(jnp.float32)))
    return (outputs[0], outputs[1], outputs[2], totals[0], totals[1], totals[2], totals[3], totals[4], totals[5], totals[6], totals[7], totals[8], totals[9], totals[10], totals[11])
```

```python
import jax
import jax.numpy as jnp
from jax import lax
from jax.experimental import pallas as pl
from jax.experimental.pallas import tpu as pltpu
from jax.sharding import Mesh
from jax.sharding import PartitionSpec as P

HEAD_DIM = 64
AXES = ("r", "z", "c")
BF = jnp.bfloat16
F32 = jnp.float32


def mm(a, b):
    return jnp.dot(a, b, preferred_element_type=F32)


def mm_tn(a, b):
    return lax.dot_general(a, b, (((0,), (0,)), ((), ())), preferred_element_type=F32)


def mm_nt(a, b):
    return lax.dot_general(a, b, (((1,), (1,)), ((), ())), preferred_element_type=F32)


def layer_norm(v, gain, shift):
    average = jnp.mean(v, axis=-1, keepdims=True)
    centred = v - average
    variance = jnp.mean(centred * centred, axis=-1, keepdims=True)
    inverse = lax.rsqrt(variance + 1e-05)
    normed = centred * inverse
    return (normed * gain + shift).astype(BF), normed, inverse


def norm_backward(grad, normed, inverse, gain):
    gain_grad = jnp.sum(grad * normed, axis=0)
    shift_grad = jnp.sum(grad, axis=0)
    scaled = grad * gain
    projected = (
        scaled
        - jnp.mean(scaled, axis=-1, keepdims=True)
        - normed * jnp.mean(scaled * normed, axis=-1, keepdims=True)
    )
    return inverse * projected, gain_grad, shift_grad


class Links:
    def __init__(self, planes_r, planes_z):
        self.R = planes_r
        self.Z = planes_z
        self.K = planes_r.bit_length() - 1
        self.M = planes_z.bit_length() - 1
        assert planes_r == 1 << self.K and planes_z == 1 << self.M

    def go(self, x, move):
        pairs = []
        for r in range(self.R):
            for z in range(self.Z):
                for c in range(2):
                    r2, z2, c2 = move(r, z, c)
                    pairs.append(((r * self.Z + z) * 2 + c, (r2 * self.Z + z2) * 2 + c2))
        return lax.ppermute(x, AXES, pairs)

    def to_plane(self, x):
        return self.go(x, lambda r, z, c: (z ^ r, r, c))

    def from_plane(self, x):
        return self.go(x, lambda r, z, c: (z, r ^ z, c))

    def core(self, x):
        return self.go(x, lambda r, z, c: (r, z, 1 - c))

    def bit(self, i, c):
        return i if c == 0 else self.K - 1 - i

    def step(self, x, i):
        return self.go(x, lambda r, z, c: (r ^ (1 << self.bit(i, c)), z, c))

    def same_step(self, x, i):
        return self.go(x, lambda r, z, c: (r ^ (1 << i), z, c))

    def layer_step(self, x, i):
        return self.go(x, lambda r, z, c: (r, z ^ (1 << i), c))

    def offset(self, p, c):
        return sum(1 << self.bit(i, c) for i in range(self.K) if p >> i & 1)

    def reverse(self, p):
        return sum(1 << (self.K - 1 - i) for i in range(self.K) if p >> i & 1)

    def gather(self, x, axis=0):
        for i in range(self.K):
            x = jnp.concatenate([x, self.step(x, i)], axis=axis)
        return x, self.core(x)

    def by_rank(self, blocks, r, c):
        near, far = blocks[: self.R], blocks[self.R :]
        even = [jnp.where(c == 0, n, f) for n, f in zip(near, far)]
        odd = [jnp.where(c == 0, f, n) for n, f in zip(near, far)]
        even = ordered(even, r)
        odd = ordered([odd[self.reverse(p)] for p in range(self.R)], r)
        return [b for pair in zip(even, odd) for b in pair]

    def by_distance(self, blocks, r, c):
        even = ordered(blocks[0::2], r)
        odd = ordered(blocks[1::2], r)
        odd = [odd[self.reverse(p)] for p in range(self.R)]
        near = [jnp.where(c == 0, a, b) for a, b in zip(even, odd)]
        far = [jnp.where(c == 0, b, a) for a, b in zip(even, odd)]
        return near + far

    def scatter_sum(self, near, far):
        away = self.core(far().astype(BF))
        total = near() + away.astype(F32)
        for i in reversed(range(self.K)):
            half = total.shape[0] // 2
            got = self.step(total[half:].astype(BF), i)
            total = total[:half] + got.astype(F32)
        return total

    def to_rows(self, near, far):
        w = near.shape[1]
        block = {(0, 0): near, (1, 0): self.core(far)}
        for i in reversed(range(self.K)):
            keys = sorted(block)
            half = block[keys[0]].shape[0] // 2
            got = self.step(jnp.concatenate([block[k][half:] for k in keys], axis=1), i)
            for n, (e, p) in enumerate(keys):
                block[(e, p | 1 << i)] = got[:, n * w : (n + 1) * w]
                block[(e, p)] = block[(e, p)][:half]
        order = [(0, p) for p in range(self.R)] + [(1, self.reverse(p)) for p in range(self.R)]
        return [block[k] for k in order]

    def to_heads(self, blocks):
        w = blocks[0].shape[1]
        block = {}
        for p in range(self.R):
            block[(0, p)] = blocks[p]
            block[(1, p)] = blocks[self.R + self.reverse(p)]
        for i in range(self.K):
            keys = sorted(k for k in block if k[1] >> i & 1)
            got = self.step(jnp.concatenate([block.pop(k) for k in keys], axis=1), i)
            for n, (e, p) in enumerate(keys):
                k = (e, p ^ 1 << i)
                block[k] = jnp.concatenate([block[k], got[:, n * w : (n + 1) * w]], axis=0)
        return block[(0, 0)], self.core(block[(1, 0)])

    def gather_parts(self, x):
        parts = [x]
        for i in range(self.K):
            parts = parts + [self.step(p, i) for p in parts]
        return parts

    def sum_chips(self, x):
        for i in range(self.K):
            x = x + self.same_step(x, i)
        return x

    def scatter_layers(self, blocks, z):
        for i in reversed(range(self.M)):
            n = blocks.shape[0] // 2
            bit = (z >> i) & 1
            keep = lax.dynamic_slice_in_dim(blocks, bit * n, n, 0)
            send = lax.dynamic_slice_in_dim(blocks, (1 - bit) * n, n, 0)
            got = self.layer_step(send, i)
            blocks = (keep.astype(F32) + got.astype(F32)).astype(blocks.dtype)
        return blocks[0]


def attend(q, k, v, pos, causal):
    heads = q.shape[1] // HEAD_DIM
    outs, lses = [], []
    for h in range(heads):
        cut = slice(h * HEAD_DIM, (h + 1) * HEAD_DIM)
        s = mm_nt(q[:, cut], k[:, cut]) * HEAD_DIM ** (-0.5)
        if causal:
            s = jnp.where(pos[:, None] >= pos[None, :], s, -1e30)
        m = jnp.max(s, axis=-1, keepdims=True)
        p = jnp.exp(s - m)
        t = jnp.sum(p, axis=-1, keepdims=True)
        outs.append(mm((p / t).astype(BF), v[:, cut]).astype(BF))
        lses.append(m + jnp.log(t))
    return jnp.concatenate(outs, axis=1), lses


def attend_back(q, k, v, e, lses, pos, causal):
    heads = q.shape[1] // HEAD_DIM
    dqs, dks, dvs = [], [], []
    for h in range(heads):
        cut = slice(h * HEAD_DIM, (h + 1) * HEAD_DIM)
        s = mm_nt(q[:, cut], k[:, cut]) * HEAD_DIM ** (-0.5)
        if causal:
            s = jnp.where(pos[:, None] >= pos[None, :], s, -1e30)
        p = jnp.exp(s - lses[h])
        dp = mm_nt(e[:, cut], v[:, cut])
        inner = jnp.sum(dp * p, axis=-1, keepdims=True)
        ds = (p * (dp - inner)).astype(BF)
        dqs.append((mm(ds, k[:, cut]) * HEAD_DIM ** (-0.5)).astype(BF))
        dks.append((mm_tn(ds, q[:, cut]) * HEAD_DIM ** (-0.5)).astype(BF))
        dvs.append(mm_tn(p.astype(BF), e[:, cut]).astype(BF))
    return tuple(jnp.concatenate(g, axis=1) for g in (dqs, dks, dvs))


def after(x, *what):
    return lax.optimization_barrier((x,) + what)[0]


def col_sum(v):
    return jnp.sum(v.astype(F32), axis=0)


def ordered(parts, index):
    n = len(parts)
    outs = []
    for k in range(n):
        v = parts[k]
        for d in range(1, n):
            v = jnp.where(index == d, parts[k ^ d], v)
        outs.append(v)
    return outs


def place_blocks(links, here, parts, cuts, shapes):
    R = links.R
    aligned = all(w % 128 == 0 for _, _, w, _, _ in cuts)
    if not aligned:
        outs = [jnp.zeros(shape, F32) for shape in shapes]
        for p in range(R):
            for out, start, w, e, spot in cuts:
                chip = here[0] ^ jnp.where(here[1] == 0, links.offset(p, 0), links.offset(p, 1))
                at = tuple(jnp.int32(v) for v in spot(chip, here[1] ^ e))
                piece = parts[p][:, start : start + w].astype(F32)
                outs[out] = lax.dynamic_update_slice(outs[out], piece, at)
        return outs

    def kernel(here_ref, *refs):
        ins, outs = refs[:R], refs[R:]
        core = here_ref[1]
        for p in range(R):
            chip = here_ref[0] ^ jnp.where(core == 0, links.offset(p, 0), links.offset(p, 1))
            for out, start, w, e, spot in cuts:
                row, col = spot(chip, core ^ e)
                n = ins[p].shape[0]
                row = row if isinstance(row, int) else pl.multiple_of(row, n)
                col = col if isinstance(col, int) else pl.multiple_of(col, 128)
                piece = ins[p][:, start : start + w].astype(F32)
                outs[out][pl.ds(row, n), pl.ds(col, w)] = piece

    return pl.pallas_call(
        kernel,
        out_shape=[jax.ShapeDtypeStruct(shape, F32) for shape in shapes],
        in_specs=[pl.BlockSpec(memory_space=pltpu.SMEM)]
        + [pl.BlockSpec(memory_space=pltpu.VMEM)] * R,
        out_specs=[pl.BlockSpec(memory_space=pltpu.VMEM)] * len(shapes),
        compiler_params=pltpu.CompilerParams(vmem_limit_bytes=40 << 20),
        cost_estimate=pl.CostEstimate(flops=0, transcendentals=0, bytes_accessed=12 << 20),
    )(here, *parts)


def make(R, Z):
    links = Links(R, Z)

    def on_device(
        hidden, encoded, cotangent, norm_gain, norm_bias, attn_bias, out_bias,
        self_qkv, self_out, cross_q, cross_kv, cross_out, ffn_in, ffn_in_bias, ffn_out,
    ):
        r = lax.axis_index("r")
        z = lax.axis_index("z")
        c = lax.axis_index("c")
        rank = r * 2 + c
        rows = hidden.shape[1]
        D = hidden.shape[2]
        own = self_out.shape[0]
        rank_cols = D // (2 * R)
        FF = ffn_in.shape[1]
        sub = ffn_out.shape[0] // R
        up_rows = FF // D
        quarter = D // Z
        zero = jnp.int32(0)

        x_low = links.to_plane(hidden[0])

        def chip_columns(w, width):
            cut = lax.dynamic_index_in_dim(w.reshape(own, -1, R, 2, width), r, 2, False)
            return cut.transpose(2, 0, 1, 3).reshape(2, own, -1)

        def gather_layers(cut):
            full = lax.all_gather(cut, ("z", "c"), axis=1, tiled=True)
            return lax.dynamic_index_in_dim(full, c, 0, False)

        cut_self = chip_columns(jnp.concatenate([self_qkv, self_out], axis=1), rank_cols)
        w_self = gather_layers(after(cut_self, x_low))
        self_out_part = w_self[:, 3 * rank_cols :]
        w_self = w_self[:, : 3 * rank_cols]
        cut_cross = chip_columns(jnp.concatenate([cross_q, cross_kv, cross_out], axis=1), rank_cols)
        w_cross = gather_layers(after(cut_cross, w_self))
        w_cross_q = w_cross[:, :rank_cols]
        w_cross_kv = w_cross[:, rank_cols : 3 * rank_cols]
        cross_out_part = w_cross[:, 3 * rank_cols :]
        width = Z * sub
        groups = D // width
        cut_up = lax.dynamic_index_in_dim(ffn_in.reshape(own, Z, 2, R, sub), r, 3, False)
        cut_up = cut_up.transpose(2, 0, 1, 3).reshape(2, own, width)
        cut_down = lax.dynamic_slice_in_dim(ffn_out, r * sub, sub, 0)
        cut_down = jnp.concatenate(
            [cut_down[:, g * width : (g + 1) * width] for g in range(groups)], axis=0
        ).reshape(2, own, width)
        cut_ffn = after(jnp.concatenate([cut_up, cut_down], axis=2), w_cross)
        w_ffn = lax.all_gather(cut_ffn, ("z", "c"), axis=1, tiled=True)
        w_up = lax.dynamic_index_in_dim(w_ffn[:, :, :width], c, 0, False)
        w_down = w_ffn[:, :, width:].reshape(2, Z, 2, groups // 2, sub, width)
        w_down = lax.dynamic_index_in_dim(w_down, c, 2, False)
        w_down = jnp.concatenate(
            [w_down[g // (groups // 2), :, g % (groups // 2)].reshape(width, width) for g in range(groups)],
            axis=1,
        )

        vec = jnp.concatenate(
            [norm_gain.T, norm_bias.T, attn_bias.T, out_bias.T, ffn_in_bias.reshape(up_rows, own)],
            axis=0,
        )
        vec = after(vec, x_low)
        vec = jnp.concatenate(ordered([vec, links.core(vec)], c), axis=1)
        for i in range(links.M):
            vec = jnp.concatenate(ordered([vec, links.layer_step(vec, i)], (z >> i) & 1), axis=1)
        vec = vec.astype(F32)
        gains, shifts, branch = vec[0:3], vec[3:6], vec[10:13]
        pair_bias = lax.dynamic_slice_in_dim(vec[6:10], rank * rank_cols, rank_cols, 1)
        up_bias = vec[13:].reshape(up_rows, 2 * Z, own).transpose(1, 0, 2).reshape(Z, 2, R, sub)
        up_bias = lax.dynamic_index_in_dim(up_bias, c, 1, False)
        up_bias = lax.dynamic_index_in_dim(up_bias, r, 1, False).reshape(width)

        def chunks(core):
            first = jnp.array([links.offset(p, 0) for p in range(R)], jnp.int32)
            second = jnp.array([links.offset(p, 1) for p in range(R)], jnp.int32)
            return (jnp.where(core == 0, first, second) ^ r ^ z) * 2 + core

        pos = jnp.concatenate([chunks(c), chunks(1 - c)])
        pos = (pos[:, None] * rows + jnp.arange(rows, dtype=jnp.int32)[None, :]).reshape(-1)
        half = R * rows

        def both(f, pair):
            return f(pair[0]), f(pair[1])

        def join(pair):
            return jnp.concatenate(pair, axis=0)

        def halves(v):
            return v[:half], v[half:]

        def total_tn(x, y):
            return (mm_tn(x[0], y[0]) + mm_tn(x[1], y[1])).astype(BF)

        def plane_sum(x, w):
            return links.scatter_sum(lambda: mm_nt(x[0], w), lambda: mm_nt(x[1], w))

        def split(v):
            w = v.shape[1] // (2 * R)
            return [v[:, i * w : (i + 1) * w] for i in range(2 * R)]

        def project(c_heads, w_out):
            blocks = links.by_rank(links.to_rows(*halves(c_heads)), r, c)
            rows_all = jnp.concatenate(blocks, axis=1)
            near, far = mm(rows_all, w_out[0]), mm(rows_all, w_out[1])
            return jnp.concatenate(links.by_rank(split_half(near) + split_half(far), r, c), axis=1)

        def split_half(v):
            return [v[:, i * rank_cols : (i + 1) * rank_cols] for i in range(R)]

        def unproject(g, w_out):
            g = links.by_distance(split(g), r, c)
            near, far = jnp.concatenate(g[:R], axis=1), jnp.concatenate(g[R:], axis=1)
            e = (mm_nt(near, w_out[0]) + mm_nt(far, w_out[1])).astype(BF)
            return links.to_heads(links.by_distance(split(e), r, c))

        def sum_layers(g):
            return lax.psum_scatter(g, "z", scatter_dimension=0, tiled=True)

        def to_core(g):
            n = g.shape[0] // 2
            keep = lax.dynamic_slice_in_dim(g, c * n, n, 0)
            send = lax.dynamic_slice_in_dim(g, (1 - c) * n, n, 0)
            return jnp.concatenate([keep, links.core(send)], axis=1)

        def place(parts, index, cuts, shapes):
            here = jnp.stack([index, c]).astype(jnp.int32)
            return place_blocks(links, here, parts, cuts, shapes)

        def columns(start, span, outer, w, core_first, out):
            def spot(o, j, cc):
                return o * 2 * R * w + (cc * R + j if core_first else j * 2 + cc) * w

            return [
                (out, start + e * span + o * w, w, e, lambda j, cc, o=o: (0, spot(o, j, cc)))
                for o in range(outer)
                for e in range(2)
            ]

        x = x_low.astype(F32)
        a1, n1, i1 = layer_norm(x, gains[0], shifts[0])
        a1 = links.gather(a1)
        memory = links.to_plane(after(encoded[0], a1[0]))
        joined = join(both(lambda v: mm(v, w_self), a1))
        q1 = (joined[:, :rank_cols] + pair_bias[0]).astype(BF)
        k1 = joined[:, rank_cols : 2 * rank_cols].astype(BF)
        v1 = (joined[:, 2 * rank_cols :] + pair_bias[1]).astype(BF)
        c1, l1 = attend(q1, k1, v1, pos, True)
        w_self_out = links.gather(after(self_out_part, a1[1]), axis=1)
        h1 = x + (project(c1, w_self_out) + branch[0])
        a2, n2, i2 = layer_norm(h1, gains[1], shifts[1])
        memory_all = links.gather(after(memory, w_self_out[0]))
        joined = join(both(lambda v: mm(v, w_cross_kv), memory_all))
        k2 = joined[:, :rank_cols].astype(BF)
        v2 = (joined[:, rank_cols:] + pair_bias[3]).astype(BF)
        a2 = links.gather(a2)
        q2 = (join(both(lambda v: mm(v, w_cross_q), a2)) + pair_bias[2]).astype(BF)
        c2, l2 = attend(q2, k2, v2, pos, False)
        seed_low = links.to_plane(after(cotangent[0], a2[0]))
        seed = seed_low.astype(F32)
        w_cross_out = links.gather(after(cross_out_part, q2), axis=1)
        h2 = h1 + (project(c2, w_cross_out) + branch[1])
        a3, n3, i3 = layer_norm(h2, gains[2], shifts[2])
        seed_all = links.gather(after(seed_low, w_cross_out[0]))
        a3 = links.gather(a3)

        def feed(v, s):
            pre = mm(v, w_up) + up_bias
            cdf = 0.5 * (1.0 + lax.erf(pre * (0.5 ** 0.5)))
            slope = cdf + pre * (jnp.exp(-0.5 * pre * pre) * (0.5 / jnp.pi) ** 0.5)
            return (pre * cdf).astype(BF), (slope * mm_nt(s, w_down)).astype(BF)

        fed = [feed(a3[0], seed_all[0]), feed(a3[1], seed_all[1])]
        act = fed[0][0], fed[1][0]
        gz = fed[0][1], fed[1][1]

        lifted, s3, t3 = norm_backward(plane_sum(gz, w_up), n3, i3, gains[2])
        down_grad = total_tn(act, seed_all)
        up_grad = total_tn(a3, gz)
        d2 = seed + lifted
        g2 = d2.astype(BF)
        e2 = unproject(g2, w_cross_out)
        gq2, gk2, gv2 = attend_back(q2, k2, v2, join(e2), l2, pos, False)
        g2_all = links.gather(after(g2, e2[1]))
        output = (h2 + (plane_sum(act, after(w_down, g2_all[0]).T) + branch[2])).astype(BF)
        output = links.from_plane(output)
        cross_out_grad = total_tn(halves(c2), g2_all)
        pair2 = jnp.concatenate([gk2, gv2], axis=1)
        cross_grad = jnp.concatenate(
            [total_tn(a2, halves(gq2)), total_tn(memory_all, halves(pair2))], axis=1
        )
        lifted, s2, t2 = norm_backward(plane_sum(halves(gq2), w_cross_q), n2, i2, gains[1])
        d1 = d2 + lifted
        g1 = d1.astype(BF)
        e1 = unproject(g1, w_self_out)
        up_width, cross_width = width, 3 * rank_cols
        g = sum_layers(jnp.concatenate([up_grad, cross_grad], axis=1))
        pack = to_core(g)
        down = sum_layers(down_grad)
        span = up_width + cross_width
        cuts = columns(0, span, Z, sub, True, 0) + columns(up_width, span, 3, rank_cols, False, 1)
        shapes = [(own, FF), (own, 3 * D)]
        down_shape = (R * sub, D)
        if sub == own:
            pack = jnp.concatenate([pack, down], axis=1)
            cuts.append((2, 2 * span, D, 0, lambda j, cc: (j * sub, 0)))
            down_parts = []
        else:
            down_parts = links.gather_parts(after(down, e1[1]))
        parts = links.gather_parts(after(pack, e1[1]))

        gq1, gk1, gv1 = attend_back(q1, k1, v1, join(e1), l1, pos, True)
        g1_all = links.gather(after(g1, e1[1]))
        encoded_grad = links.from_plane(plane_sum(halves(after(pair2, g1_all[0])), w_cross_kv).astype(BF))
        self_out_grad = total_tn(halves(c1), g1_all)
        triple = after(jnp.concatenate([gq1, gk1, gv1], axis=1), *parts)
        self_grad = total_tn(a1, halves(triple))
        lifted, s1, t1 = norm_backward(plane_sum(halves(triple), w_self), n1, i1, gains[0])
        hidden_grad = links.from_plane((d1 + lifted).astype(BF))

        if sub == own:
            ffn_in_grad, cross_both, ffn_out_grad = place(parts, r, cuts, shapes + [down_shape])
        else:
            ffn_in_grad, cross_both = place(parts, r, cuts, shapes)
            cuts = [(0, 0, D, 0, lambda j, cc: (j * sub, 0))]
            (ffn_out_grad,) = place(down_parts, r, cuts, [down_shape])
        cross_q_grad = cross_both[:, :D]
        cross_kv_grad = cross_both[:, D:]
        pack = to_core(sum_layers(self_grad))
        (self_qkv_grad,) = place(
            links.gather_parts(pack),
            r,
            columns(0, 3 * rank_cols, 3, rank_cols, False, 0),
            [(own, 3 * D)],
        )
        g = jnp.concatenate([cross_out_grad, self_out_grad], axis=0)
        g = g.reshape(2 * rank_cols, Z, quarter).transpose(1, 0, 2)
        g = links.to_plane(links.scatter_layers(g, z))
        (both_out,) = place(
            links.gather_parts(g),
            r ^ z,
            [(0, 0, quarter, 0, lambda j, cc: (0, j * quarter))],
            [(2 * rank_cols, D)],
        )
        cross_out_grad, self_out_grad = both_out[:rank_cols], both_out[rank_cols:]

        def sum_small(v):
            k = v.shape[0]
            blocks = v.reshape(k, Z, 2, own).transpose(2, 1, 0, 3)
            away = lax.dynamic_index_in_dim(blocks, 1 - c, 0, False)
            near = lax.dynamic_index_in_dim(blocks, c, 0, False) + links.core(away)
            return links.sum_chips(links.scatter_layers(near, z))

        def spread(v):
            return lax.dynamic_update_slice(
                jnp.zeros((v.shape[0], D), F32), v, (zero, rank * rank_cols)
            )

        up_sums = (col_sum(gz[0]) + col_sum(gz[1])).reshape(Z, 1, 1, sub)
        up_sums = lax.dynamic_update_slice(jnp.zeros((Z, 2, R, sub), F32), up_sums, (zero, c, r, zero))
        up_sums = up_sums.reshape(2 * Z, up_rows, own).transpose(1, 0, 2).reshape(up_rows, D)
        sums = jnp.concatenate(
            [
                jnp.stack([s1, s2, s3, t1, t2, t3]),
                spread(jnp.stack([col_sum(gq1), col_sum(gv1), col_sum(gq2), col_sum(gv2)])),
                jnp.stack([col_sum(g1), col_sum(g2), col_sum(seed_low)]),
                up_sums,
            ],
            axis=0,
        )
        sums = sum_small(after(sums, hidden_grad))
        return (
            output[None],
            hidden_grad.astype(F32)[None],
            encoded_grad.astype(F32)[None],
            sums[0:3].T,
            sums[3:6].T,
            sums[6:10].T,
            sums[10:13].T,
            self_qkv_grad,
            self_out_grad,
            cross_q_grad,
            cross_kv_grad,
            cross_out_grad,
            ffn_in_grad,
            sums[13:].reshape(-1),
            ffn_out_grad,
        )

    return on_device


def solution(mesh):
    R = mesh.shape["replica"]
    Z = mesh.shape["shard"] // 2
    inner = Mesh(mesh.devices.reshape(R, Z, 2), AXES)
    rows = P("r", ("z", "c"), None)
    weight = P(("z", "c"), None)
    line = P(("z", "c"))
    return jax.shard_map(
        make(R, Z),
        mesh=inner,
        in_specs=(rows,) * 3 + (weight,) * 10 + (line, weight),
        out_specs=(rows,) * 3 + (weight,) * 10 + (line, weight),
        check_vma=False,
    )
```

```python
import jax
import jax.numpy as jnp
from jax import lax
from jax.experimental import pallas as pl
from jax.experimental.pallas import tpu as pltpu
from jax.sharding import Mesh
from jax.sharding import PartitionSpec as P

HEAD_DIM = 64
AXES = ("r", "z", "c")
BF = jnp.bfloat16
F32 = jnp.float32


def mm(a, b):
    return jnp.dot(a, b, preferred_element_type=F32)


def mm_tn(a, b):
    return lax.dot_general(a, b, (((0,), (0,)), ((), ())), preferred_element_type=F32)


def mm_nt(a, b):
    return lax.dot_general(a, b, (((1,), (1,)), ((), ())), preferred_element_type=F32)


def layer_norm(v, gain, shift):
    average = jnp.mean(v, axis=-1, keepdims=True)
    centred = v - average
    variance = jnp.mean(centred * centred, axis=-1, keepdims=True)
    inverse = lax.rsqrt(variance + 1e-05)
    normed = centred * inverse
    return (normed * gain + shift).astype(BF), normed, inverse


def norm_backward(grad, normed, inverse, gain):
    gain_grad = jnp.sum(grad * normed, axis=0)
    shift_grad = jnp.sum(grad, axis=0)
    scaled = grad * gain
    projected = (
        scaled
        - jnp.mean(scaled, axis=-1, keepdims=True)
        - normed * jnp.mean(scaled * normed, axis=-1, keepdims=True)
    )
    return inverse * projected, gain_grad, shift_grad


class Links:
    def __init__(self, planes_r, planes_z):
        self.R = planes_r
        self.Z = planes_z
        self.K = planes_r.bit_length() - 1
        self.M = planes_z.bit_length() - 1
        assert planes_r == 1 << self.K and planes_z == 1 << self.M

    def go(self, x, move):
        pairs = []
        for r in range(self.R):
            for z in range(self.Z):
                for c in range(2):
                    r2, z2, c2 = move(r, z, c)
                    pairs.append(((r * self.Z + z) * 2 + c, (r2 * self.Z + z2) * 2 + c2))
        return lax.ppermute(x, AXES, pairs)

    def to_plane(self, x):
        return self.go(x, lambda r, z, c: (z ^ r, r, c))

    def from_plane(self, x):
        return self.go(x, lambda r, z, c: (z, r ^ z, c))

    def core(self, x):
        return self.go(x, lambda r, z, c: (r, z, 1 - c))

    def bit(self, i, c):
        return i if c == 0 else self.K - 1 - i

    def step(self, x, i):
        return self.go(x, lambda r, z, c: (r ^ (1 << self.bit(i, c)), z, c))

    def same_step(self, x, i):
        return self.go(x, lambda r, z, c: (r ^ (1 << i), z, c))

    def layer_step(self, x, i):
        return self.go(x, lambda r, z, c: (r, z ^ (1 << i), c))

    def offset(self, p, c):
        return sum(1 << self.bit(i, c) for i in range(self.K) if p >> i & 1)

    def reverse(self, p):
        return sum(1 << (self.K - 1 - i) for i in range(self.K) if p >> i & 1)

    def gather(self, *xs):
        xs = list(xs)
        for i in range(self.K):
            n = xs[0].shape[0]
            got = self.step(jnp.concatenate(xs, axis=0) if len(xs) > 1 else xs[0], i)
            got = [got[k * n : (k + 1) * n] for k in range(len(xs))]
            if i < self.K - 1:
                xs = [jnp.concatenate([x, g], axis=0) for x, g in zip(xs, got)]
        far = [(self.core(x), self.core(g)) for x, g in zip(xs, got)]
        out = [(x, g) + f for x, g, f in zip(xs, got, far)]
        return out if len(out) > 1 else out[0]

    def scatter_sum(self, term):
        part = {}
        for k in (1, 0):
            away = self.core(term(2 + k).astype(BF))
            part[k] = term(k) + away.astype(F32)
        total = part[0] + self.step(part[1].astype(BF), self.K - 1).astype(F32)
        for i in reversed(range(self.K - 1)):
            n = total.shape[0] // 2
            total = total[:n] + self.step(total[n:].astype(BF), i).astype(F32)
        return total

    def gather_parts(self, x):
        parts = [x]
        for i in range(self.K):
            parts = parts + [self.step(p, i) for p in parts]
        return parts

    def sum_chips(self, x):
        for i in range(self.K):
            x = x + self.same_step(x, i)
        return x

    def scatter_layers(self, blocks, z):
        for i in reversed(range(self.M)):
            n = blocks.shape[0] // 2
            bit = (z >> i) & 1
            keep = lax.dynamic_slice_in_dim(blocks, bit * n, n, 0)
            send = lax.dynamic_slice_in_dim(blocks, (1 - bit) * n, n, 0)
            got = self.layer_step(send, i)
            blocks = (keep.astype(F32) + got.astype(F32)).astype(blocks.dtype)
        return blocks[0]


def attend(q, k, v, pos, causal):
    heads = q.shape[1] // HEAD_DIM
    outs, lses = [], []
    for h in range(heads):
        cut = slice(h * HEAD_DIM, (h + 1) * HEAD_DIM)
        s = mm_nt(q[:, cut], k[:, cut]) * HEAD_DIM ** (-0.5)
        if causal:
            s = jnp.where(pos[:, None] >= pos[None, :], s, -1e30)
        m = jnp.max(s, axis=-1, keepdims=True)
        p = jnp.exp(s - m)
        t = jnp.sum(p, axis=-1, keepdims=True)
        outs.append(mm((p / t).astype(BF), v[:, cut]).astype(BF))
        lses.append(m + jnp.log(t))
    return jnp.concatenate(outs, axis=1), lses


def attend_back(q, k, v, e, lses, pos, causal):
    heads = q.shape[1] // HEAD_DIM
    dqs, dks, dvs = [], [], []
    for h in range(heads):
        cut = slice(h * HEAD_DIM, (h + 1) * HEAD_DIM)
        s = mm_nt(q[:, cut], k[:, cut]) * HEAD_DIM ** (-0.5)
        if causal:
            s = jnp.where(pos[:, None] >= pos[None, :], s, -1e30)
        p = jnp.exp(s - lses[h])
        dp = mm_nt(e[:, cut], v[:, cut])
        inner = jnp.sum(dp * p, axis=-1, keepdims=True)
        ds = (p * (dp - inner)).astype(BF)
        dqs.append((mm(ds, k[:, cut]) * HEAD_DIM ** (-0.5)).astype(BF))
        dks.append((mm_tn(ds, q[:, cut]) * HEAD_DIM ** (-0.5)).astype(BF))
        dvs.append(mm_tn(p.astype(BF), e[:, cut]).astype(BF))
    return tuple(jnp.concatenate(g, axis=1) for g in (dqs, dks, dvs))


def after(x, *what):
    return lax.optimization_barrier((x,) + what)[0]


def col_sum(v):
    return jnp.sum(v.astype(F32), axis=0)


def ordered(parts, index):
    n = len(parts)
    outs = []
    for k in range(n):
        v = parts[k]
        for d in range(1, n):
            v = jnp.where(index == d, parts[k ^ d], v)
        outs.append(v)
    return outs


def pick_ffn(core, gathered, Z, own, sub, width, groups):
    half = groups // 2

    def kernel(core_ref, in_ref, up_ref, down_ref):
        core = core_ref[0]
        for s in range(2 * Z):
            up_ref[pl.ds(s * own, own)] = in_ref[core, pl.ds(s * 2 * own, own)]
        for z in range(Z):
            for g in range(groups):
                row = pl.multiple_of((z * 2 + core) * 2 * own + own + (g % half) * sub, 16)
                piece = in_ref[g // half, pl.ds(row, sub)]
                down_ref[pl.ds(z * sub, sub), pl.ds(g * width, width)] = piece

    D = gathered.shape[1] // 2
    vmem = pl.BlockSpec(memory_space=pltpu.VMEM)
    return pl.pallas_call(
        kernel,
        out_shape=[jax.ShapeDtypeStruct((D, width), BF), jax.ShapeDtypeStruct((width, D), BF)],
        in_specs=[pl.BlockSpec(memory_space=pltpu.SMEM), vmem],
        out_specs=[vmem, vmem],
        compiler_params=pltpu.CompilerParams(vmem_limit_bytes=24 << 20),
        cost_estimate=pl.CostEstimate(flops=0, transcendentals=0, bytes_accessed=8 << 20),
    )(core, gathered)


def place_ffn(core, gathered, R, Z, own, sub, width, groups):
    D = groups * width
    shapes = [(own, 2 * R * width), (R * sub, D)]
    gathered = gathered.reshape(R, 2, 2 * own, 2 * width)
    if sub % 128 != 0:
        up = lax.dynamic_slice_in_dim(gathered, core[0] * own, own, 2)[..., :width]
        up = up.reshape(R, 2, own, Z, sub).transpose(2, 3, 1, 0, 4).reshape(shapes[0])
        down = lax.dynamic_index_in_dim(gathered, core[0], 1, False)[..., width:]
        down = down.reshape(R, groups, sub, width).transpose(0, 2, 1, 3).reshape(shapes[1])
        return up.astype(F32), down.astype(F32)

    def kernel(core_ref, in_ref, up_ref, down_ref):
        me = core_ref[0]
        rows = pl.ds(pl.multiple_of(me * own, own), own)
        for j in range(R):
            for cc in range(2):
                for o in range(Z):
                    col = ((o * 2 + cc) * R + j) * sub
                    piece = in_ref[j, cc, rows, pl.ds(o * sub, sub)]
                    up_ref[:, pl.ds(col, sub)] = piece.astype(F32)
            for g in range(groups):
                piece = in_ref[j, me, pl.ds(g * sub, sub), pl.ds(width, width)]
                down_ref[pl.ds(j * sub, sub), pl.ds(g * width, width)] = piece.astype(F32)

    vmem = pl.BlockSpec(memory_space=pltpu.VMEM)
    return pl.pallas_call(
        kernel,
        out_shape=[jax.ShapeDtypeStruct(shape, F32) for shape in shapes],
        in_specs=[pl.BlockSpec(memory_space=pltpu.SMEM), vmem],
        out_specs=[vmem, vmem],
        compiler_params=pltpu.CompilerParams(vmem_limit_bytes=32 << 20),
        cost_estimate=pl.CostEstimate(flops=0, transcendentals=0, bytes_accessed=8 << 20),
    )(core, gathered)


def place_blocks(links, here, parts, cuts, shapes):
    R = links.R
    aligned = all(w % 128 == 0 for _, _, w, _, _ in cuts)
    if not aligned:
        outs = [jnp.zeros(shape, F32) for shape in shapes]
        for p in range(R):
            for out, start, w, e, spot in cuts:
                chip = here[0] ^ jnp.where(here[1] == 0, links.offset(p, 0), links.offset(p, 1))
                at = tuple(jnp.int32(v) for v in spot(chip, here[1] ^ e))
                piece = parts[p][:, start : start + w].astype(F32)
                outs[out] = lax.dynamic_update_slice(outs[out], piece, at)
        return outs

    def kernel(here_ref, *refs):
        ins, outs = refs[:R], refs[R:]
        core = here_ref[1]
        for p in range(R):
            chip = here_ref[0] ^ jnp.where(core == 0, links.offset(p, 0), links.offset(p, 1))
            for out, start, w, e, spot in cuts:
                row, col = spot(chip, core ^ e)
                n = ins[p].shape[0]
                row = row if isinstance(row, int) else pl.multiple_of(row, n)
                col = col if isinstance(col, int) else pl.multiple_of(col, 128)
                piece = ins[p][:, start : start + w].astype(F32)
                outs[out][pl.ds(row, n), pl.ds(col, w)] = piece

    return pl.pallas_call(
        kernel,
        out_shape=[jax.ShapeDtypeStruct(shape, F32) for shape in shapes],
        in_specs=[pl.BlockSpec(memory_space=pltpu.SMEM)]
        + [pl.BlockSpec(memory_space=pltpu.VMEM)] * R,
        out_specs=[pl.BlockSpec(memory_space=pltpu.VMEM)] * len(shapes),
        compiler_params=pltpu.CompilerParams(vmem_limit_bytes=40 << 20),
        cost_estimate=pl.CostEstimate(flops=0, transcendentals=0, bytes_accessed=12 << 20),
    )(here, *parts)


def make(R, Z):
    links = Links(R, Z)

    def on_device(
        hidden, encoded, cotangent, norm_gain, norm_bias, attn_bias, out_bias,
        self_qkv, self_out, cross_q, cross_kv, cross_out, ffn_in, ffn_in_bias, ffn_out,
    ):
        r = lax.axis_index("r")
        z = lax.axis_index("z")
        c = lax.axis_index("c")
        rank = r * 2 + c
        rows = hidden.shape[1]
        D = hidden.shape[2]
        own = self_out.shape[0]
        rank_cols = D // (2 * R)
        FF = ffn_in.shape[1]
        sub = ffn_out.shape[0] // R
        up_rows = FF // D
        quarter = D // Z
        zero = jnp.int32(0)

        x_low = links.to_plane(hidden[0])

        def chip_columns(w, width):
            cut = lax.dynamic_index_in_dim(w.reshape(own, -1, R, 2, width), r, 2, False)
            return cut.transpose(2, 0, 1, 3).reshape(2, own, -1)

        def gather_layers(cut):
            full = lax.all_gather(cut, ("z", "c"), axis=1, tiled=True)
            return lax.dynamic_index_in_dim(full, c, 0, False)

        w_out = jnp.concatenate([self_out, cross_out], axis=0)
        w_out = lax.dynamic_slice_in_dim(w_out, (r ^ z) * quarter, quarter, 1)
        w_out = links.from_plane(w_out).reshape(2, own, quarter)
        cut_self = jnp.concatenate([chip_columns(self_qkv, rank_cols), w_out], axis=2)
        w_self = lax.all_gather(after(cut_self, x_low), ("z", "c"), axis=1, tiled=True)
        w_out = w_self[:, :, 3 * rank_cols :].reshape(2, Z, 2, own, quarter)
        w_out = lax.dynamic_index_in_dim(w_out, c, 2, False)
        w_self_out = jnp.concatenate([w_out[0, i] for i in range(Z)], axis=1)
        w_cross_out = jnp.concatenate([w_out[1, i] for i in range(Z)], axis=1)
        w_self = lax.dynamic_index_in_dim(w_self[:, :, : 3 * rank_cols], c, 0, False)
        cut_cross = chip_columns(jnp.concatenate([cross_q, cross_kv], axis=1), rank_cols)
        w_cross = gather_layers(after(cut_cross, x_low))
        w_cross_q = w_cross[:, :rank_cols]
        w_cross_kv = w_cross[:, rank_cols:]
        width = Z * sub
        groups = D // width
        cut_up = lax.dynamic_index_in_dim(ffn_in.reshape(own, Z, 2, R, sub), r, 3, False)
        cut_up = cut_up.transpose(2, 0, 1, 3).reshape(2, own, width)
        cut_down = lax.dynamic_slice_in_dim(ffn_out, r * sub, sub, 0)
        cut_down = jnp.concatenate(
            [cut_down[:, g * width : (g + 1) * width] for g in range(groups)], axis=0
        ).reshape(2, own, width)
        cut_ffn = after(jnp.concatenate([cut_up, cut_down], axis=1), x_low)
        w_ffn = lax.all_gather(cut_ffn, ("z", "c"), axis=1, tiled=True)
        w_up, w_down = pick_ffn(jnp.stack([c]).astype(jnp.int32), w_ffn, Z, own, sub, width, groups)

        vec = jnp.concatenate(
            [norm_gain.T, norm_bias.T, attn_bias.T, out_bias.T, ffn_in_bias.reshape(up_rows, own)],
            axis=0,
        )
        vec = after(vec, x_low)
        vec = jnp.concatenate(ordered([vec, links.core(vec)], c), axis=1)
        for i in range(links.M):
            vec = jnp.concatenate(ordered([vec, links.layer_step(vec, i)], (z >> i) & 1), axis=1)
        vec = vec.astype(F32)
        gains, shifts, branch = vec[0:3], vec[3:6], vec[10:13]
        pair_bias = lax.dynamic_slice_in_dim(vec[6:10], rank * rank_cols, rank_cols, 1)
        up_bias = vec[13:].reshape(up_rows, 2 * Z, own).transpose(1, 0, 2).reshape(Z, 2, R, sub)
        up_bias = lax.dynamic_index_in_dim(up_bias, c, 1, False)
        up_bias = lax.dynamic_index_in_dim(up_bias, r, 1, False).reshape(width)

        def chunks(core):
            first = jnp.array([links.offset(p, 0) for p in range(R)], jnp.int32)
            second = jnp.array([links.offset(p, 1) for p in range(R)], jnp.int32)
            return (jnp.where(core == 0, first, second) ^ r ^ z) * 2 + core

        pos = jnp.concatenate([chunks(c), chunks(1 - c)])
        pos = (pos[:, None] * rows + jnp.arange(rows, dtype=jnp.int32)[None, :]).reshape(-1)
        piece = R * rows // 2

        def each(f, pieces):
            return [f(v) for v in pieces]

        def join(pieces):
            return jnp.concatenate(pieces, axis=0)

        def cut4(v):
            return [v[k * piece : (k + 1) * piece] for k in range(4)]

        def total_tn(x, y):
            return mm_tn(join(x), join(y)).astype(BF)

        def plane_sum(x, w, product=mm_nt):
            return links.scatter_sum(lambda k: product(x[k], w))

        def sum_layers(g):
            return lax.psum_scatter(g, "z", scatter_dimension=0, tiled=True)

        def to_core(g):
            n = g.shape[0] // 2
            keep = lax.dynamic_slice_in_dim(g, c * n, n, 0)
            send = lax.dynamic_slice_in_dim(g, (1 - c) * n, n, 0)
            return jnp.concatenate([keep, links.core(send)], axis=1)

        def place(parts, index, cuts, shapes):
            here = jnp.stack([index, c]).astype(jnp.int32)
            return place_blocks(links, here, parts, cuts, shapes)

        def columns(start, span, outer, w, core_first, out):
            def spot(o, j, cc):
                return o * 2 * R * w + (cc * R + j if core_first else j * 2 + cc) * w

            return [
                (out, start + e * span + o * w, w, e, lambda j, cc, o=o: (0, spot(o, j, cc)))
                for o in range(outer)
                for e in range(2)
            ]

        x = x_low.astype(F32)
        a1, n1, i1 = layer_norm(x, gains[0], shifts[0])
        a1 = links.gather(a1)
        memory = links.to_plane(after(encoded[0], w_self))
        joined = each(lambda v: mm(v, w_self), a1)
        q1 = join([(v[:, :rank_cols] + pair_bias[0]).astype(BF) for v in joined])
        k1 = join([v[:, rank_cols : 2 * rank_cols].astype(BF) for v in joined])
        v1 = join([(v[:, 2 * rank_cols :] + pair_bias[1]).astype(BF) for v in joined])
        c1, l1 = attend(q1, k1, v1, pos, True)
        c1 = cut4(after(c1, memory))
        h1 = after(x + (plane_sum(c1, w_self_out, mm) + branch[0]), w_cross)
        a2, n2, i2 = layer_norm(h1, gains[1], shifts[1])
        seed_low = links.to_plane(after(cotangent[0], a2))
        seed = seed_low.astype(F32)
        a2, memory_all = links.gather(a2, memory)
        joined = each(lambda v: mm(v, w_cross_kv), memory_all)
        k2 = join([v[:, :rank_cols].astype(BF) for v in joined])
        v2 = join([(v[:, rank_cols:] + pair_bias[3]).astype(BF) for v in joined])
        q2 = join([(mm(v, w_cross_q) + pair_bias[2]).astype(BF) for v in a2])
        c2, l2 = attend(after(q2, seed_low), k2, v2, pos, False)
        c2 = cut4(after(c2, w_up, w_down))
        h2 = h1 + (plane_sum(c2, w_cross_out, mm) + branch[1])
        a3, n3, i3 = layer_norm(h2, gains[2], shifts[2])
        a3, seed_all = links.gather(a3, seed_low)

        def feed(v, s):
            pre = mm(v, w_up) + up_bias
            cdf = 0.5 * (1.0 + lax.erf(pre * (0.5 ** 0.5)))
            slope = cdf + pre * (jnp.exp(-0.5 * pre * pre) * (0.5 / jnp.pi) ** 0.5)
            return (pre * cdf).astype(BF), (slope * mm_nt(s, w_down)).astype(BF)

        fed = [feed(a3[k], seed_all[k]) for k in range(4)]
        act = [f[0] for f in fed]
        gz = [f[1] for f in fed]

        lifted, s3, t3 = norm_backward(plane_sum(gz, w_up), n3, i3, gains[2])
        act_all, seed_rows = join(act), join(seed_all)
        down_grad = [
            mm_tn(act_all, seed_rows[:, g * width : (g + 1) * width]).astype(BF).reshape(Z, sub, width)
            for g in range(groups)
        ]
        down_grad = jnp.stack(down_grad, axis=1).reshape(D, width)
        ffn_grad = jnp.concatenate([total_tn(a3, gz), down_grad], axis=1)
        d2 = after(seed + lifted, ffn_grad)
        ffn_grad = sum_layers(ffn_grad)
        g2 = d2.astype(BF)
        g2_all = links.gather(g2)
        e2 = join([mm_nt(v, w_cross_out).astype(BF) for v in g2_all])
        gq2, gk2, gv2 = attend_back(q2, k2, v2, e2, l2, pos, False)
        output = (h2 + (plane_sum(act, after(w_down, g2_all[0]), mm) + branch[2])).astype(BF)
        cross_out_grad = total_tn(c2, g2_all)
        pair2 = jnp.concatenate([gk2, gv2], axis=1)
        cross_grad = jnp.concatenate(
            [mm_tn(join(a2), gq2).astype(BF), mm_tn(join(memory_all), pair2).astype(BF)], axis=1
        )
        lifted, s2, t2 = norm_backward(plane_sum(cut4(gq2), w_cross_q), n2, i2, gains[1])
        output = links.from_plane(output)
        d1 = after(d2 + lifted, cross_grad, cross_out_grad, ffn_grad, output)
        g1 = d1.astype(BF)
        g1_all = links.gather(g1)
        e1 = join([mm_nt(v, w_self_out).astype(BF) for v in g1_all])
        gq1, gk1, gv1 = attend_back(q1, k1, v1, e1, l1, pos, True)
        encoded_grad = plane_sum(cut4(after(pair2, g1_all[0])), w_cross_kv).astype(BF)

        ffn_all = lax.all_gather(ffn_grad, ("r", "c"), axis=0, tiled=True)
        ffn_in_grad, ffn_out_grad = place_ffn(
            jnp.stack([c]).astype(jnp.int32), ffn_all, R, Z, own, sub, width, groups
        )
        triple = after(jnp.concatenate([gq1, gk1, gv1], axis=1), encoded_grad)
        self_grad = mm_tn(join(a1), triple).astype(BF)
        self_out_grad = total_tn(c1, g1_all)
        triple = after(triple, self_grad)
        lifted, s1, t1 = norm_backward(plane_sum(cut4(triple), w_self), n1, i1, gains[0])
        encoded_grad = links.from_plane(encoded_grad)
        hidden_grad = links.from_plane((after(d1, encoded_grad, ffn_in_grad) + lifted).astype(BF))

        out_grad = jnp.concatenate([cross_out_grad, self_out_grad], axis=0)
        out_grad = out_grad.reshape(2 * rank_cols, Z, quarter).transpose(1, 0, 2).reshape(D, quarter)
        span = 6 * rank_cols
        pack = sum_layers(jnp.concatenate([cross_grad, self_grad, out_grad], axis=1))
        out_grad = pack[:, span:]
        pack = links.gather_parts(to_core(after(pack[:, :span], hidden_grad)))
        cross_both, self_qkv_grad = place(
            pack,
            r,
            columns(0, span, 3, rank_cols, False, 0)
            + columns(3 * rank_cols, span, 3, rank_cols, False, 1),
            [(own, 3 * D), (own, 3 * D)],
        )
        cross_q_grad = cross_both[:, :D]
        cross_kv_grad = cross_both[:, D:]
        out_parts = links.gather_parts(links.to_plane(after(out_grad, hidden_grad)))
        (both_out,) = place(
            out_parts,
            r ^ z,
            [(0, 0, quarter, 0, lambda j, cc: (0, j * quarter))],
            [(2 * rank_cols, D)],
        )
        cross_out_grad, self_out_grad = both_out[:rank_cols], both_out[rank_cols:]

        def sum_small(v):
            k = v.shape[0]
            blocks = v.reshape(k, Z, 2, own).transpose(2, 1, 0, 3)
            away = lax.dynamic_index_in_dim(blocks, 1 - c, 0, False)
            near = lax.dynamic_index_in_dim(blocks, c, 0, False) + links.core(away)
            return links.sum_chips(links.scatter_layers(near, z))

        def spread(v):
            return lax.dynamic_update_slice(
                jnp.zeros((v.shape[0], D), F32), v, (zero, rank * rank_cols)
            )

        up_sums = sum(col_sum(v) for v in gz).reshape(Z, 1, 1, sub)
        up_sums = lax.dynamic_update_slice(jnp.zeros((Z, 2, R, sub), F32), up_sums, (zero, c, r, zero))
        up_sums = up_sums.reshape(2 * Z, up_rows, own).transpose(1, 0, 2).reshape(up_rows, D)
        sums = jnp.concatenate(
            [
                jnp.stack([s1, s2, s3, t1, t2, t3]),
                spread(jnp.stack([col_sum(gq1), col_sum(gv1), col_sum(gq2), col_sum(gv2)])),
                jnp.stack([col_sum(g1), col_sum(g2), col_sum(seed_low)]),
                up_sums,
            ],
            axis=0,
        )
        sums = sum_small(after(sums, hidden_grad))
        return (
            output[None],
            hidden_grad.astype(F32)[None],
            encoded_grad.astype(F32)[None],
            sums[0:3].T,
            sums[3:6].T,
            sums[6:10].T,
            sums[10:13].T,
            self_qkv_grad,
            self_out_grad,
            cross_q_grad,
            cross_kv_grad,
            cross_out_grad,
            ffn_in_grad,
            sums[13:].reshape(-1),
            ffn_out_grad,
        )

    return on_device


def solution(mesh):
    R = mesh.shape["replica"]
    Z = mesh.shape["shard"] // 2
    inner = Mesh(mesh.devices.reshape(R, Z, 2), AXES)
    rows = P("r", ("z", "c"), None)
    weight = P(("z", "c"), None)
    line = P(("z", "c"))
    return jax.shard_map(
        make(R, Z),
        mesh=inner,
        in_specs=(rows,) * 3 + (weight,) * 10 + (line, weight),
        out_specs=(rows,) * 3 + (weight,) * 10 + (line, weight),
        check_vma=False,
    )
```

```python
import jax
import jax.numpy as jnp
from jax import lax
from jax.experimental import pallas as pl
from jax.experimental.layout import Layout, with_layout_constraint
from jax.experimental.pallas import tpu as pltpu
from jax.sharding import Mesh
from jax.sharding import PartitionSpec as P

HEAD_DIM = 64
AXES = ("r", "z", "c")
BF = jnp.bfloat16
F32 = jnp.float32


def mm(a, b):
    return jnp.dot(a, b, preferred_element_type=F32)


def mm_tn(a, b):
    return lax.dot_general(a, b, (((0,), (0,)), ((), ())), preferred_element_type=F32)


def mm_nt(a, b):
    return lax.dot_general(a, b, (((1,), (1,)), ((), ())), preferred_element_type=F32)


def layer_norm(v, gain, shift):
    average = jnp.mean(v, axis=-1, keepdims=True)
    centred = v - average
    variance = jnp.mean(centred * centred, axis=-1, keepdims=True)
    inverse = lax.rsqrt(variance + 1e-05)
    normed = centred * inverse
    return (normed * gain + shift).astype(BF), normed, inverse


def norm_backward(grad, normed, inverse, gain):
    gain_grad = jnp.sum(grad * normed, axis=0)
    shift_grad = jnp.sum(grad, axis=0)
    scaled = grad * gain
    projected = (
        scaled
        - jnp.mean(scaled, axis=-1, keepdims=True)
        - normed * jnp.mean(scaled * normed, axis=-1, keepdims=True)
    )
    return inverse * projected, gain_grad, shift_grad


class Links:
    def __init__(self, planes_r, planes_z):
        self.R = planes_r
        self.Z = planes_z
        self.K = planes_r.bit_length() - 1
        self.M = planes_z.bit_length() - 1
        assert planes_r == 1 << self.K and planes_z == 1 << self.M

    def go(self, x, move):
        pairs = []
        for r in range(self.R):
            for z in range(self.Z):
                for c in range(2):
                    r2, z2, c2 = move(r, z, c)
                    pairs.append(((r * self.Z + z) * 2 + c, (r2 * self.Z + z2) * 2 + c2))
        return lax.ppermute(x, AXES, pairs)

    def to_plane(self, x):
        return self.go(x, lambda r, z, c: (z ^ r, r, c))

    def from_plane(self, x):
        return self.go(x, lambda r, z, c: (z, r ^ z, c))

    def core(self, x):
        return self.go(x, lambda r, z, c: (r, z, 1 - c))

    def bit(self, i, c):
        return i if c == 0 else self.K - 1 - i

    def step(self, x, i):
        return self.go(x, lambda r, z, c: (r ^ (1 << self.bit(i, c)), z, c))

    def same_step(self, x, i):
        return self.go(x, lambda r, z, c: (r ^ (1 << i), z, c))

    def layer_step(self, x, i):
        return self.go(x, lambda r, z, c: (r, z ^ (1 << i), c))

    def offset(self, p, c):
        return sum(1 << self.bit(i, c) for i in range(self.K) if p >> i & 1)

    def reverse(self, p):
        return sum(1 << (self.K - 1 - i) for i in range(self.K) if p >> i & 1)

    def gather(self, *xs):
        xs = list(xs)
        for i in range(self.K):
            n = xs[0].shape[0]
            got = self.step(jnp.concatenate(xs, axis=0) if len(xs) > 1 else xs[0], i)
            got = [got[k * n : (k + 1) * n] for k in range(len(xs))]
            if i < self.K - 1:
                xs = [jnp.concatenate([x, g], axis=0) for x, g in zip(xs, got)]
        far = [(self.core(x), self.core(g)) for x, g in zip(xs, got)]
        out = [(x, g) + f for x, g, f in zip(xs, got, far)]
        return out if len(out) > 1 else out[0]

    def scatter_sum(self, term):
        part = {}
        for k in (1, 0):
            away = self.core(term(2 + k).astype(BF))
            part[k] = term(k) + away.astype(F32)
        total = part[0] + self.step(part[1].astype(BF), self.K - 1).astype(F32)
        for i in reversed(range(self.K - 1)):
            n = total.shape[0] // 2
            total = total[:n] + self.step(total[n:].astype(BF), i).astype(F32)
        return total

    def spread_chips(self, blocks):
        held = [(p, b) for p, b in enumerate(blocks)]
        for i in range(self.K):
            away = [m for m, (left, _) in enumerate(held) if left >> i & 1]
            n = held[0][1].shape[0]
            got = self.step(jnp.concatenate([held[m][1] for m in away], axis=0), i)
            for k, m in enumerate(away):
                held[m] = (held[m][0] ^ 1 << i, got[k * n : (k + 1) * n])
        return [b for _, b in held]

    def gather_parts(self, x):
        parts = [x]
        for i in range(self.K):
            parts = parts + [self.step(p, i) for p in parts]
        return parts

    def sum_chips(self, x):
        for i in range(self.K):
            x = x + self.same_step(x, i)
        return x

    def scatter_layers(self, blocks, z):
        for i in reversed(range(self.M)):
            n = blocks.shape[0] // 2
            bit = (z >> i) & 1
            keep = lax.dynamic_slice_in_dim(blocks, bit * n, n, 0)
            send = lax.dynamic_slice_in_dim(blocks, (1 - bit) * n, n, 0)
            got = self.layer_step(send, i)
            blocks = (keep.astype(F32) + got.astype(F32)).astype(blocks.dtype)
        return blocks[0]


def attend(q, k, v, pos, causal):
    heads = q.shape[1] // HEAD_DIM
    outs, lses = [], []
    for h in range(heads):
        cut = slice(h * HEAD_DIM, (h + 1) * HEAD_DIM)
        s = mm_nt(q[:, cut], k[:, cut]) * HEAD_DIM ** (-0.5)
        if causal:
            s = jnp.where(pos[:, None] >= pos[None, :], s, -1e30)
        m = jnp.max(s, axis=-1, keepdims=True)
        p = jnp.exp(s - m)
        t = jnp.sum(p, axis=-1, keepdims=True)
        outs.append(mm((p / t).astype(BF), v[:, cut]).astype(BF))
        lses.append(m + jnp.log(t))
    return jnp.concatenate(outs, axis=1), lses


def attend_back(q, k, v, e, context, lses, pos, causal):
    heads = q.shape[1] // HEAD_DIM
    dqs, dks, dvs = [], [], []
    for h in range(heads):
        cut = slice(h * HEAD_DIM, (h + 1) * HEAD_DIM)
        s = mm_nt(q[:, cut], k[:, cut]) * HEAD_DIM ** (-0.5)
        if causal:
            s = jnp.where(pos[:, None] >= pos[None, :], s, -1e30)
        p = jnp.exp(s - lses[h])
        dp = mm_nt(e[:, cut], v[:, cut])
        inner = jnp.sum(e[:, cut].astype(F32) * context[:, cut].astype(F32), axis=-1, keepdims=True)
        ds = (p * (dp - inner)).astype(BF)
        dqs.append((mm(ds, k[:, cut]) * HEAD_DIM ** (-0.5)).astype(BF))
        dks.append((mm_tn(ds, q[:, cut]) * HEAD_DIM ** (-0.5)).astype(BF))
        dvs.append(mm_tn(p.astype(BF), e[:, cut]).astype(BF))
    return tuple(jnp.concatenate(g, axis=1) for g in (dqs, dks, dvs))


def after(x, *what):
    return lax.optimization_barrier((x,) + what)[0]


def col_sum(v):
    return jnp.sum(v.astype(F32), axis=0)


def ordered(parts, index):
    n = len(parts)
    outs = []
    for k in range(n):
        v = parts[k]
        for d in range(1, n):
            v = jnp.where(index == d, parts[k ^ d], v)
        outs.append(v)
    return outs


def pick_ffn(core, gathered, Z, own, sub, width, groups):
    half = groups // 2

    def kernel(core_ref, in_ref, up_ref, down_ref):
        core = core_ref[0]
        for s in range(2 * Z):
            up_ref[pl.ds(s * own, own)] = in_ref[core, pl.ds(s * 2 * own, own)]
        for z in range(Z):
            for g in range(groups):
                row = pl.multiple_of((z * 2 + core) * 2 * own + own + (g % half) * sub, 16)
                piece = in_ref[g // half, pl.ds(row, sub)]
                down_ref[pl.ds(z * sub, sub), pl.ds(g * width, width)] = piece

    D = gathered.shape[1] // 2
    vmem = pl.BlockSpec(memory_space=pltpu.VMEM)
    return pl.pallas_call(
        kernel,
        out_shape=[jax.ShapeDtypeStruct((D, width), BF), jax.ShapeDtypeStruct((width, D), BF)],
        in_specs=[pl.BlockSpec(memory_space=pltpu.SMEM), vmem],
        out_specs=[vmem, vmem],
        compiler_params=pltpu.CompilerParams(vmem_limit_bytes=24 << 20),
        cost_estimate=pl.CostEstimate(flops=0, transcendentals=0, bytes_accessed=8 << 20),
    )(core, gathered)


def place_ffn(core, gathered, R, Z, own, sub, width, groups):
    D = groups * width
    shapes = [(own, 2 * R * width), (R * sub, D)]
    gathered = gathered.reshape(R, 2, 2 * own, 2 * width)
    if sub % 128 != 0:
        up = lax.dynamic_slice_in_dim(gathered, core[0] * own, own, 2)[..., :width]
        up = up.reshape(R, 2, own, Z, sub).transpose(2, 3, 1, 0, 4).reshape(shapes[0])
        down = lax.dynamic_index_in_dim(gathered, core[0], 1, False)[..., width:]
        down = down.reshape(R, groups, sub, width).transpose(0, 2, 1, 3).reshape(shapes[1])
        return up.astype(F32), down.astype(F32)

    def kernel(core_ref, in_ref, up_ref, down_ref):
        me = core_ref[0]
        rows = pl.ds(pl.multiple_of(me * own, own), own)
        for j in range(R):
            for cc in range(2):
                for o in range(Z):
                    col = ((o * 2 + cc) * R + j) * sub
                    piece = in_ref[j, cc, rows, pl.ds(o * sub, sub)]
                    up_ref[:, pl.ds(col, sub)] = piece.astype(F32)
            for g in range(groups):
                piece = in_ref[j, me, pl.ds(g * sub, sub), pl.ds(width, width)]
                down_ref[pl.ds(j * sub, sub), pl.ds(g * width, width)] = piece.astype(F32)

    vmem = pl.BlockSpec(memory_space=pltpu.VMEM)
    return pl.pallas_call(
        kernel,
        out_shape=[jax.ShapeDtypeStruct(shape, F32) for shape in shapes],
        in_specs=[pl.BlockSpec(memory_space=pltpu.SMEM), vmem],
        out_specs=[vmem, vmem],
        compiler_params=pltpu.CompilerParams(vmem_limit_bytes=32 << 20),
        cost_estimate=pl.CostEstimate(flops=0, transcendentals=0, bytes_accessed=8 << 20),
    )(core, gathered)


def place_blocks(links, here, parts, cuts, shapes):
    R = links.R
    aligned = all(w % 128 == 0 for _, _, w, _, _ in cuts)
    if not aligned:
        outs = [jnp.zeros(shape, F32) for shape in shapes]
        for p in range(R):
            for out, start, w, e, spot in cuts:
                chip = here[0] ^ jnp.where(here[1] == 0, links.offset(p, 0), links.offset(p, 1))
                at = tuple(jnp.int32(v) for v in spot(chip, here[1] ^ e))
                piece = parts[p][:, start : start + w].astype(F32)
                outs[out] = lax.dynamic_update_slice(outs[out], piece, at)
        return outs

    def kernel(here_ref, *refs):
        ins, outs = refs[:R], refs[R:]
        core = here_ref[1]
        for p in range(R):
            chip = here_ref[0] ^ jnp.where(core == 0, links.offset(p, 0), links.offset(p, 1))
            for out, start, w, e, spot in cuts:
                row, col = spot(chip, core ^ e)
                n = ins[p].shape[0]
                row = row if isinstance(row, int) else pl.multiple_of(row, n)
                col = col if isinstance(col, int) else pl.multiple_of(col, 128)
                piece = ins[p][:, start : start + w].astype(F32)
                outs[out][pl.ds(row, n), pl.ds(col, w)] = piece

    return pl.pallas_call(
        kernel,
        out_shape=[jax.ShapeDtypeStruct(shape, F32) for shape in shapes],
        in_specs=[pl.BlockSpec(memory_space=pltpu.SMEM)]
        + [pl.BlockSpec(memory_space=pltpu.VMEM)] * R,
        out_specs=[pl.BlockSpec(memory_space=pltpu.VMEM)] * len(shapes),
        compiler_params=pltpu.CompilerParams(vmem_limit_bytes=40 << 20),
        cost_estimate=pl.CostEstimate(flops=0, transcendentals=0, bytes_accessed=12 << 20),
    )(here, *parts)


def make(R, Z):
    links = Links(R, Z)

    def on_device(
        hidden, encoded, cotangent, norm_gain, norm_bias, attn_bias, out_bias,
        self_qkv, self_out, cross_q, cross_kv, cross_out, ffn_in, ffn_in_bias, ffn_out,
    ):
        r = lax.axis_index("r")
        z = lax.axis_index("z")
        c = lax.axis_index("c")
        rank = r * 2 + c
        rows = hidden.shape[1]
        D = hidden.shape[2]
        own = self_out.shape[0]
        rank_cols = D // (2 * R)
        FF = ffn_in.shape[1]
        sub = ffn_out.shape[0] // R
        up_rows = FF // D
        quarter = D // Z
        zero = jnp.int32(0)

        x_low = links.to_plane(hidden[0])

        def chip_columns(w, width):
            cut = lax.dynamic_index_in_dim(w.reshape(own, -1, R, 2, width), r, 2, False)
            return cut.transpose(2, 0, 1, 3).reshape(2, own, -1)

        def gather_layers(cut):
            full = lax.all_gather(cut, ("z", "c"), axis=1, tiled=True)
            return lax.dynamic_index_in_dim(full, c, 0, False)

        w_out = jnp.concatenate([self_out, cross_out], axis=0)
        w_out = lax.dynamic_slice_in_dim(w_out, (r ^ z) * quarter, quarter, 1)
        w_out = links.from_plane(w_out).reshape(2, own, quarter)
        cut_self = jnp.concatenate([chip_columns(self_qkv, rank_cols), w_out], axis=2)
        w_self = lax.all_gather(after(cut_self, x_low), ("z", "c"), axis=1, tiled=True)
        w_out = w_self[:, :, 3 * rank_cols :].reshape(2, Z, 2, own, quarter)
        w_out = lax.dynamic_index_in_dim(w_out, c, 2, False)
        w_self_out = jnp.concatenate([w_out[0, i] for i in range(Z)], axis=1)
        w_cross_out = jnp.concatenate([w_out[1, i] for i in range(Z)], axis=1)
        w_self = lax.dynamic_index_in_dim(w_self[:, :, : 3 * rank_cols], c, 0, False)
        cut_cross = chip_columns(jnp.concatenate([cross_q, cross_kv], axis=1), rank_cols)
        w_cross = gather_layers(after(cut_cross, x_low))
        w_cross_q = w_cross[:, :rank_cols]
        w_cross_kv = w_cross[:, rank_cols:]
        width = Z * sub
        groups = D // width
        cut_up = lax.dynamic_index_in_dim(ffn_in.reshape(own, Z, 2, R, sub), r, 3, False)
        cut_up = cut_up.transpose(2, 0, 1, 3).reshape(2, own, width)
        cut_down = lax.dynamic_slice_in_dim(ffn_out, r * sub, sub, 0)
        cut_down = jnp.concatenate(
            [cut_down[:, g * width : (g + 1) * width] for g in range(groups)], axis=0
        ).reshape(2, own, width)
        cut_ffn = after(jnp.concatenate([cut_up, cut_down], axis=1), x_low)
        w_ffn = lax.all_gather(cut_ffn, ("z", "c"), axis=1, tiled=True)
        w_up, w_down = pick_ffn(jnp.stack([c]).astype(jnp.int32), w_ffn, Z, own, sub, width, groups)

        vec = jnp.concatenate(
            [norm_gain.T, norm_bias.T, attn_bias.T, out_bias.T, ffn_in_bias.reshape(up_rows, own)],
            axis=0,
        )
        vec = after(vec, x_low)
        vec = jnp.concatenate(ordered([vec, links.core(vec)], c), axis=1)
        for i in range(links.M):
            vec = jnp.concatenate(ordered([vec, links.layer_step(vec, i)], (z >> i) & 1), axis=1)
        vec = vec.astype(F32)
        gains, shifts, branch = vec[0:3], vec[3:6], vec[10:13]
        pair_bias = lax.dynamic_slice_in_dim(vec[6:10], rank * rank_cols, rank_cols, 1)
        up_bias = vec[13:].reshape(up_rows, 2 * Z, own).transpose(1, 0, 2).reshape(Z, 2, R, sub)
        up_bias = lax.dynamic_index_in_dim(up_bias, c, 1, False)
        up_bias = lax.dynamic_index_in_dim(up_bias, r, 1, False).reshape(width)

        def chunks(core):
            first = jnp.array([links.offset(p, 0) for p in range(R)], jnp.int32)
            second = jnp.array([links.offset(p, 1) for p in range(R)], jnp.int32)
            return (jnp.where(core == 0, first, second) ^ r ^ z) * 2 + core

        pos = jnp.concatenate([chunks(c), chunks(1 - c)])
        pos = (pos[:, None] * rows + jnp.arange(rows, dtype=jnp.int32)[None, :]).reshape(-1)
        piece = R * rows // 2

        def each(f, pieces):
            return [f(v) for v in pieces]

        def join(pieces):
            return jnp.concatenate(pieces, axis=0)

        def cut4(v):
            return [v[k * piece : (k + 1) * piece] for k in range(4)]

        def total_tn(x, y):
            return mm_tn(join(x), join(y)).astype(BF)

        def plane_sum(x, w, product=mm_nt):
            return links.scatter_sum(lambda k: product(x[k], w))

        def sum_layers(g):
            return lax.psum_scatter(g, "z", scatter_dimension=0, tiled=True)

        def to_core(g):
            n = g.shape[0] // 2
            keep = lax.dynamic_slice_in_dim(g, c * n, n, 0)
            send = lax.dynamic_slice_in_dim(g, (1 - c) * n, n, 0)
            return jnp.concatenate([keep, links.core(send)], axis=1)

        def place(parts, index, cuts, shapes):
            here = jnp.stack([index, c]).astype(jnp.int32)
            return place_blocks(links, here, parts, cuts, shapes)

        def columns(start, span, outer, w, core_first, out):
            def spot(o, j, cc):
                return o * 2 * R * w + (cc * R + j if core_first else j * 2 + cc) * w

            return [
                (out, start + e * span + o * w, w, e, lambda j, cc, o=o: (0, spot(o, j, cc)))
                for o in range(outer)
                for e in range(2)
            ]

        x = x_low.astype(F32)
        a1, n1, i1 = layer_norm(x, gains[0], shifts[0])
        a1 = links.gather(a1)
        memory = links.to_plane(after(encoded[0], w_self))
        joined = each(lambda v: mm(v, w_self), a1)
        q1 = join([(v[:, :rank_cols] + pair_bias[0]).astype(BF) for v in joined])
        k1 = join([v[:, rank_cols : 2 * rank_cols].astype(BF) for v in joined])
        v1 = join([(v[:, 2 * rank_cols :] + pair_bias[1]).astype(BF) for v in joined])
        c1, l1 = attend(q1, k1, v1, pos, True)
        c1 = cut4(after(c1, memory))
        h1 = after(x + (plane_sum(c1, w_self_out, mm) + branch[0]), w_cross)
        a2, n2, i2 = layer_norm(h1, gains[1], shifts[1])
        seed_low = links.to_plane(after(cotangent[0], a2))
        seed = seed_low.astype(F32)
        a2, memory_all = links.gather(a2, memory)
        joined = each(lambda v: mm(v, w_cross_kv), memory_all)
        k2 = join([v[:, :rank_cols].astype(BF) for v in joined])
        v2 = join([(v[:, rank_cols:] + pair_bias[3]).astype(BF) for v in joined])
        q2 = join([(mm(v, w_cross_q) + pair_bias[2]).astype(BF) for v in a2])
        c2, l2 = attend(after(q2, seed_low), k2, v2, pos, False)
        c2 = cut4(after(c2, w_up, w_down))
        h2 = h1 + (plane_sum(c2, w_cross_out, mm) + branch[1])
        a3, n3, i3 = layer_norm(h2, gains[2], shifts[2])
        a3, seed_all = links.gather(a3, seed_low)

        def feed(v, s):
            pre = mm(v, w_up) + up_bias
            cdf = 0.5 * (1.0 + lax.erf(pre * (0.5 ** 0.5)))
            slope = cdf + pre * (jnp.exp(-0.5 * pre * pre) * (0.5 / jnp.pi) ** 0.5)
            return (pre * cdf).astype(BF), (slope * mm_nt(s, w_down)).astype(BF)

        fed = [feed(a3[k], seed_all[k]) for k in range(4)]
        act = [f[0] for f in fed]
        gz = [f[1] for f in fed]

        lifted, s3, t3 = norm_backward(plane_sum(gz, w_up), n3, i3, gains[2])
        act_all, seed_rows = join(act), join(seed_all)
        down_grad = [
            mm_tn(act_all, seed_rows[:, g * width : (g + 1) * width]).astype(BF).reshape(Z, sub, width)
            for g in range(groups)
        ]
        down_grad = jnp.stack(down_grad, axis=1).reshape(D, width)
        ffn_grad = jnp.concatenate([total_tn(a3, gz), down_grad], axis=1)
        d2 = seed + lifted
        ffn_grad = sum_layers(ffn_grad)
        g2 = d2.astype(BF)
        g2_all = links.gather(g2)
        e2 = join([mm_nt(v, w_cross_out).astype(BF) for v in g2_all])
        gq2, gk2, gv2 = attend_back(q2, k2, v2, e2, join(c2), l2, pos, False)
        output = (h2 + (plane_sum(act, after(w_down, g2_all[0]), mm) + branch[2])).astype(BF)
        cross_out_grad = total_tn(c2, g2_all)
        pair2 = jnp.concatenate([gk2, gv2], axis=1)
        cross_grad = jnp.concatenate(
            [mm_tn(join(a2), gq2).astype(BF), mm_tn(join(memory_all), pair2).astype(BF)], axis=1
        )
        lifted, s2, t2 = norm_backward(plane_sum(cut4(gq2), w_cross_q), n2, i2, gains[1])
        d1 = after(d2 + lifted, cross_grad, cross_out_grad, ffn_grad, output)
        g1 = d1.astype(BF)
        g1_all = links.gather(g1)
        e1 = join([mm_nt(v, w_self_out).astype(BF) for v in g1_all])
        gq1, gk1, gv1 = attend_back(q1, k1, v1, e1, join(c1), l1, pos, True)
        encoded_grad = plane_sum(cut4(after(pair2, g1_all[3])), w_cross_kv).astype(BF)

        ffn_grad = with_layout_constraint(ffn_grad, Layout((0, 1)))
        ffn_all = lax.all_gather(ffn_grad, ("r", "c"), axis=0, tiled=True)
        ffn_in_grad, ffn_out_grad = place_ffn(
            jnp.stack([c]).astype(jnp.int32), ffn_all, R, Z, own, sub, width, groups
        )
        output = links.from_plane(output)
        triple = after(jnp.concatenate([gq1, gk1, gv1], axis=1), encoded_grad, output)
        self_grad = mm_tn(join(a1), triple).astype(BF)
        self_out_grad = total_tn(c1, g1_all)
        out_grad = jnp.concatenate([cross_out_grad, self_out_grad], axis=0)
        far_chip = [jnp.where(c == 0, links.offset(p, 0), links.offset(p, 1)) for p in range(R)]
        out_grad = links.spread_chips(
            [lax.dynamic_slice_in_dim(out_grad, (r ^ f) * quarter, quarter, 1) for f in far_chip]
        )
        turned = [out_grad[links.reverse(p)] for p in range(R)]
        out_grad = ordered([jnp.where(c == 0, p, t) for p, t in zip(out_grad, turned)], r)
        out_grad = lax.optimization_barrier(jnp.concatenate(lax.optimization_barrier(out_grad), axis=0))
        triple = after(triple, self_grad)
        lifted, s1, t1 = norm_backward(plane_sum(cut4(triple), w_self), n1, i1, gains[0])
        hidden_grad = links.from_plane((after(d1, ffn_in_grad) + lifted).astype(BF))
        encoded_grad = links.from_plane(after(encoded_grad, hidden_grad))

        span = 6 * rank_cols
        pack = sum_layers(jnp.concatenate([cross_grad, self_grad, out_grad], axis=1))
        pack = after(pack, hidden_grad)
        out_grad = pack[:, span:]
        pack = [to_core(pack[:, :span]), out_grad[:own], out_grad[own:]]
        parts = links.gather_parts(jnp.concatenate(pack, axis=1))
        cross_both, self_qkv_grad = place(
            parts,
            r,
            columns(0, span, 3, rank_cols, False, 0)
            + columns(3 * rank_cols, span, 3, rank_cols, False, 1),
            [(own, 3 * D), (own, 3 * D)],
        )
        cross_q_grad = cross_both[:, :D]
        cross_kv_grad = cross_both[:, D:]
        cross_out_grad, self_out_grad = place(
            parts,
            r,
            [(i, 2 * span + i * quarter, quarter, 0, lambda j, cc: (0, j * quarter)) for i in range(2)],
            [(own, D), (own, D)],
        )

        def sum_small(v):
            k = v.shape[0]
            blocks = v.reshape(k, Z, 2, own).transpose(2, 1, 0, 3)
            away = lax.dynamic_index_in_dim(blocks, 1 - c, 0, False)
            near = lax.dynamic_index_in_dim(blocks, c, 0, False) + links.core(away)
            return links.sum_chips(links.scatter_layers(near, z))

        def spread(v):
            return lax.dynamic_update_slice(
                jnp.zeros((v.shape[0], D), F32), v, (zero, rank * rank_cols)
            )

        up_sums = sum(col_sum(v) for v in gz).reshape(Z, 1, 1, sub)
        up_sums = lax.dynamic_update_slice(jnp.zeros((Z, 2, R, sub), F32), up_sums, (zero, c, r, zero))
        up_sums = up_sums.reshape(2 * Z, up_rows, own).transpose(1, 0, 2).reshape(up_rows, D)
        sums = jnp.concatenate(
            [
                jnp.stack([s1, s2, s3, t1, t2, t3]),
                spread(jnp.stack([col_sum(gq1), col_sum(gv1), col_sum(gq2), col_sum(gv2)])),
                jnp.stack([col_sum(g1), col_sum(g2), col_sum(seed_low)]),
                up_sums,
            ],
            axis=0,
        )
        sums = sum_small(after(sums, hidden_grad))
        return (
            output[None],
            hidden_grad.astype(F32)[None],
            encoded_grad.astype(F32)[None],
            sums[0:3].T,
            sums[3:6].T,
            sums[6:10].T,
            sums[10:13].T,
            self_qkv_grad,
            self_out_grad,
            cross_q_grad,
            cross_kv_grad,
            cross_out_grad,
            ffn_in_grad,
            sums[13:].reshape(-1),
            ffn_out_grad,
        )

    return on_device


def solution(mesh):
    R = mesh.shape["replica"]
    Z = mesh.shape["shard"] // 2
    inner = Mesh(mesh.devices.reshape(R, Z, 2), AXES)
    rows = P("r", ("z", "c"), None)
    weight = P(("z", "c"), None)
    line = P(("z", "c"))
    return jax.shard_map(
        make(R, Z),
        mesh=inner,
        in_specs=(rows,) * 3 + (weight,) * 10 + (line, weight),
        out_specs=(rows,) * 3 + (weight,) * 10 + (line, weight),
        check_vma=False,
    )
```

```python
import jax
import jax.numpy as jnp
from jax import lax
from jax.experimental import pallas as pl
from jax.experimental.pallas import tpu as pltpu
from jax.sharding import Mesh
from jax.sharding import PartitionSpec as P

HEAD_DIM = 64
AXES = ("r", "z", "c")
BF = jnp.bfloat16
F32 = jnp.float32


def mm(a, b):
    return jnp.dot(a, b, preferred_element_type=F32)


def mm_tn(a, b):
    return lax.dot_general(a, b, (((0,), (0,)), ((), ())), preferred_element_type=F32)


def mm_nt(a, b):
    return lax.dot_general(a, b, (((1,), (1,)), ((), ())), preferred_element_type=F32)


def layer_norm(v, gain, shift):
    average = jnp.mean(v, axis=-1, keepdims=True)
    centred = v - average
    variance = jnp.mean(centred * centred, axis=-1, keepdims=True)
    inverse = lax.rsqrt(variance + 1e-05)
    normed = centred * inverse
    return (normed * gain + shift).astype(BF), normed, inverse


def norm_backward(grad, normed, inverse, gain):
    gain_grad = jnp.sum(grad * normed, axis=0)
    shift_grad = jnp.sum(grad, axis=0)
    scaled = grad * gain
    projected = (
        scaled
        - jnp.mean(scaled, axis=-1, keepdims=True)
        - normed * jnp.mean(scaled * normed, axis=-1, keepdims=True)
    )
    return inverse * projected, gain_grad, shift_grad


class Links:
    def __init__(self, planes_r, planes_z):
        self.R = planes_r
        self.Z = planes_z
        self.K = planes_r.bit_length() - 1
        self.M = planes_z.bit_length() - 1
        assert planes_r == 1 << self.K and planes_z == 1 << self.M

    def go(self, x, move):
        pairs = []
        for r in range(self.R):
            for z in range(self.Z):
                for c in range(2):
                    r2, z2, c2 = move(r, z, c)
                    pairs.append(((r * self.Z + z) * 2 + c, (r2 * self.Z + z2) * 2 + c2))
        return lax.ppermute(x, AXES, pairs)

    def to_plane(self, x):
        return self.go(x, lambda r, z, c: (z ^ r, r, c))

    def from_plane(self, x):
        return self.go(x, lambda r, z, c: (z, r ^ z, c))

    def core(self, x):
        return self.go(x, lambda r, z, c: (r, z, 1 - c))

    def bit(self, i, c):
        return i if c == 0 else self.K - 1 - i

    def step(self, x, i):
        return self.go(x, lambda r, z, c: (r ^ (1 << self.bit(i, c)), z, c))

    def same_step(self, x, i):
        return self.go(x, lambda r, z, c: (r ^ (1 << i), z, c))

    def layer_step(self, x, i):
        return self.go(x, lambda r, z, c: (r, z ^ (1 << i), c))

    def offset(self, p, c):
        return sum(1 << self.bit(i, c) for i in range(self.K) if p >> i & 1)

    def reverse(self, p):
        return sum(1 << (self.K - 1 - i) for i in range(self.K) if p >> i & 1)

    def gather(self, *xs):
        xs = list(xs)
        for i in range(self.K):
            n = xs[0].shape[0]
            got = self.step(jnp.concatenate(xs, axis=0) if len(xs) > 1 else xs[0], i)
            got = [got[k * n : (k + 1) * n] for k in range(len(xs))]
            if i < self.K - 1:
                xs = [jnp.concatenate([x, g], axis=0) for x, g in zip(xs, got)]
        far = [(self.core(x), self.core(g)) for x, g in zip(xs, got)]
        out = [(x, g) + f for x, g, f in zip(xs, got, far)]
        return out if len(out) > 1 else out[0]

    def scatter_sum(self, term):
        part = {}
        for k in (1, 0):
            away = self.core(term(2 + k).astype(BF))
            part[k] = term(k) + away.astype(F32)
        total = part[0] + self.step(part[1].astype(BF), self.K - 1).astype(F32)
        for i in reversed(range(self.K - 1)):
            n = total.shape[0] // 2
            total = total[:n] + self.step(total[n:].astype(BF), i).astype(F32)
        return total

    def spread_chips(self, blocks):
        held = [(p, b) for p, b in enumerate(blocks)]
        for i in range(self.K):
            away = [m for m, (left, _) in enumerate(held) if left >> i & 1]
            n = held[0][1].shape[0]
            got = self.step(jnp.concatenate([held[m][1] for m in away], axis=0), i)
            for k, m in enumerate(away):
                held[m] = (held[m][0] ^ 1 << i, got[k * n : (k + 1) * n])
        return [b for _, b in held]

    def gather_parts(self, x):
        parts = [x]
        for i in range(self.K):
            parts = parts + [self.step(p, i) for p in parts]
        return parts

    def sum_chips(self, x):
        for i in range(self.K):
            x = x + self.same_step(x, i)
        return x

    def scatter_layers(self, blocks, z):
        for i in reversed(range(self.M)):
            n = blocks.shape[0] // 2
            bit = (z >> i) & 1
            keep = lax.dynamic_slice_in_dim(blocks, bit * n, n, 0)
            send = lax.dynamic_slice_in_dim(blocks, (1 - bit) * n, n, 0)
            got = self.layer_step(send, i)
            blocks = (keep.astype(F32) + got.astype(F32)).astype(blocks.dtype)
        return blocks[0]


def attend(q, k, v, pos, causal):
    heads = q.shape[1] // HEAD_DIM
    outs, lses = [], []
    for h in range(heads):
        cut = slice(h * HEAD_DIM, (h + 1) * HEAD_DIM)
        s = mm_nt(q[:, cut], k[:, cut]) * HEAD_DIM ** (-0.5)
        if causal:
            s = jnp.where(pos[:, None] >= pos[None, :], s, -1e30)
        m = jnp.max(s, axis=-1, keepdims=True)
        p = jnp.exp(s - m)
        t = jnp.sum(p, axis=-1, keepdims=True)
        outs.append(mm((p / t).astype(BF), v[:, cut]).astype(BF))
        lses.append(m + jnp.log(t))
    return jnp.concatenate(outs, axis=1), lses


def attend_back(q, k, v, e, context, lses, pos, causal):
    heads = q.shape[1] // HEAD_DIM
    dqs, dks, dvs = [], [], []
    for h in range(heads):
        cut = slice(h * HEAD_DIM, (h + 1) * HEAD_DIM)
        s = mm_nt(q[:, cut], k[:, cut]) * HEAD_DIM ** (-0.5)
        if causal:
            s = jnp.where(pos[:, None] >= pos[None, :], s, -1e30)
        p = jnp.exp(s - lses[h])
        dp = mm_nt(e[:, cut], v[:, cut])
        inner = jnp.sum(e[:, cut].astype(F32) * context[:, cut].astype(F32), axis=-1, keepdims=True)
        ds = (p * (dp - inner)).astype(BF)
        dqs.append((mm(ds, k[:, cut]) * HEAD_DIM ** (-0.5)).astype(BF))
        dks.append((mm_tn(ds, q[:, cut]) * HEAD_DIM ** (-0.5)).astype(BF))
        dvs.append(mm_tn(p.astype(BF), e[:, cut]).astype(BF))
    return tuple(jnp.concatenate(g, axis=1) for g in (dqs, dks, dvs))


def after(x, *what):
    return lax.optimization_barrier((x,) + what)[0]


def col_sum(v):
    return jnp.sum(v.astype(F32), axis=0)


def ordered(parts, index):
    n = len(parts)
    outs = []
    for k in range(n):
        v = parts[k]
        for d in range(1, n):
            v = jnp.where(index == d, parts[k ^ d], v)
        outs.append(v)
    return outs


def pick_ffn(core, gathered, Z, own, sub, width, groups):
    half = groups // 2

    def kernel(core_ref, in_ref, up_ref, down_ref):
        core = core_ref[0]
        for s in range(2 * Z):
            up_ref[pl.ds(s * own, own)] = in_ref[core, pl.ds(s * 2 * own, own)]
        for z in range(Z):
            for g in range(groups):
                row = pl.multiple_of((z * 2 + core) * 2 * own + own + (g % half) * sub, 16)
                piece = in_ref[g // half, pl.ds(row, sub)]
                down_ref[pl.ds(z * sub, sub), pl.ds(g * width, width)] = piece

    D = gathered.shape[1] // 2
    vmem = pl.BlockSpec(memory_space=pltpu.VMEM)
    return pl.pallas_call(
        kernel,
        out_shape=[jax.ShapeDtypeStruct((D, width), BF), jax.ShapeDtypeStruct((width, D), BF)],
        in_specs=[pl.BlockSpec(memory_space=pltpu.SMEM), vmem],
        out_specs=[vmem, vmem],
        compiler_params=pltpu.CompilerParams(vmem_limit_bytes=24 << 20),
        cost_estimate=pl.CostEstimate(flops=0, transcendentals=0, bytes_accessed=8 << 20),
    )(core, gathered)


def place_blocks(links, here, parts, cuts, shapes):
    R = links.R
    aligned = all(w % 128 == 0 for _, _, w, _, _ in cuts)
    if not aligned:
        outs = [jnp.zeros(shape, F32) for shape in shapes]
        for p in range(R):
            for out, start, w, e, spot in cuts:
                chip = here[0] ^ jnp.where(here[1] == 0, links.offset(p, 0), links.offset(p, 1))
                at = tuple(jnp.int32(v) for v in spot(chip, here[1] ^ e))
                piece = parts[p][:, start : start + w].astype(F32)
                outs[out] = lax.dynamic_update_slice(outs[out], piece, at)
        return outs

    def kernel(here_ref, *refs):
        ins, outs = refs[:R], refs[R:]
        core = here_ref[1]
        for p in range(R):
            chip = here_ref[0] ^ jnp.where(core == 0, links.offset(p, 0), links.offset(p, 1))
            for out, start, w, e, spot in cuts:
                row, col = spot(chip, core ^ e)
                n = ins[p].shape[0]
                row = row if isinstance(row, int) else pl.multiple_of(row, n)
                col = col if isinstance(col, int) else pl.multiple_of(col, 128)
                piece = ins[p][:, start : start + w].astype(F32)
                outs[out][pl.ds(row, n), pl.ds(col, w)] = piece

    return pl.pallas_call(
        kernel,
        out_shape=[jax.ShapeDtypeStruct(shape, F32) for shape in shapes],
        in_specs=[pl.BlockSpec(memory_space=pltpu.SMEM)]
        + [pl.BlockSpec(memory_space=pltpu.VMEM)] * R,
        out_specs=[pl.BlockSpec(memory_space=pltpu.VMEM)] * len(shapes),
        compiler_params=pltpu.CompilerParams(vmem_limit_bytes=40 << 20),
        cost_estimate=pl.CostEstimate(flops=0, transcendentals=0, bytes_accessed=12 << 20),
    )(here, *parts)


def make(R, Z):
    links = Links(R, Z)

    def on_device(
        hidden, encoded, cotangent, norm_gain, norm_bias, attn_bias, out_bias,
        self_qkv, self_out, cross_q, cross_kv, cross_out, ffn_in, ffn_in_bias, ffn_out,
    ):
        r = lax.axis_index("r")
        z = lax.axis_index("z")
        c = lax.axis_index("c")
        rank = r * 2 + c
        rows = hidden.shape[1]
        D = hidden.shape[2]
        own = self_out.shape[0]
        rank_cols = D // (2 * R)
        FF = ffn_in.shape[1]
        sub = ffn_out.shape[0] // R
        up_rows = FF // D
        quarter = D // Z
        zero = jnp.int32(0)

        x_low = links.to_plane(hidden[0])

        def chip_columns(w, width):
            cut = lax.dynamic_index_in_dim(w.reshape(own, -1, R, 2, width), r, 2, False)
            return cut.transpose(2, 0, 1, 3).reshape(2, own, -1)

        def gather_layers(cut):
            full = lax.all_gather(cut, ("z", "c"), axis=1, tiled=True)
            return lax.dynamic_index_in_dim(full, c, 0, False)

        w_out = jnp.concatenate([self_out, cross_out], axis=0)
        w_out = lax.dynamic_slice_in_dim(w_out, (r ^ z) * quarter, quarter, 1)
        w_out = links.from_plane(w_out).reshape(2, own, quarter)
        cut_self = jnp.concatenate([chip_columns(self_qkv, rank_cols), w_out], axis=2)
        w_self = lax.all_gather(after(cut_self, x_low), ("z", "c"), axis=1, tiled=True)
        w_out = w_self[:, :, 3 * rank_cols :].reshape(2, Z, 2, own, quarter)
        w_out = lax.dynamic_index_in_dim(w_out, c, 2, False)
        w_self_out = jnp.concatenate([w_out[0, i] for i in range(Z)], axis=1)
        w_cross_out = jnp.concatenate([w_out[1, i] for i in range(Z)], axis=1)
        w_self = lax.dynamic_index_in_dim(w_self[:, :, : 3 * rank_cols], c, 0, False)
        cut_cross = chip_columns(jnp.concatenate([cross_q, cross_kv], axis=1), rank_cols)
        w_cross = gather_layers(after(cut_cross, x_low))
        w_cross_q = w_cross[:, :rank_cols]
        w_cross_kv = w_cross[:, rank_cols:]
        width = Z * sub
        groups = D // width
        cut_up = lax.dynamic_index_in_dim(ffn_in.reshape(own, Z, 2, R, sub), r, 3, False)
        cut_up = cut_up.transpose(2, 0, 1, 3).reshape(2, own, width)
        cut_down = lax.dynamic_slice_in_dim(ffn_out, r * sub, sub, 0)
        cut_down = jnp.concatenate(
            [cut_down[:, g * width : (g + 1) * width] for g in range(groups)], axis=0
        ).reshape(2, own, width)
        cut_ffn = after(jnp.concatenate([cut_up, cut_down], axis=1), x_low)
        w_ffn = lax.all_gather(cut_ffn, ("z", "c"), axis=1, tiled=True)
        w_up, w_down = pick_ffn(jnp.stack([c]).astype(jnp.int32), w_ffn, Z, own, sub, width, groups)

        vec = jnp.concatenate(
            [norm_gain.T, norm_bias.T, attn_bias.T, out_bias.T, ffn_in_bias.reshape(up_rows, own)],
            axis=0,
        )
        vec = after(vec, x_low)
        vec = jnp.concatenate(ordered([vec, links.core(vec)], c), axis=1)
        for i in range(links.M):
            vec = jnp.concatenate(ordered([vec, links.layer_step(vec, i)], (z >> i) & 1), axis=1)
        vec = vec.astype(F32)
        gains, shifts, branch = vec[0:3], vec[3:6], vec[10:13]
        pair_bias = lax.dynamic_slice_in_dim(vec[6:10], rank * rank_cols, rank_cols, 1)
        up_bias = vec[13:].reshape(up_rows, 2 * Z, own).transpose(1, 0, 2).reshape(Z, 2, R, sub)
        up_bias = lax.dynamic_index_in_dim(up_bias, c, 1, False)
        up_bias = lax.dynamic_index_in_dim(up_bias, r, 1, False).reshape(width)

        def chunks(core):
            first = jnp.array([links.offset(p, 0) for p in range(R)], jnp.int32)
            second = jnp.array([links.offset(p, 1) for p in range(R)], jnp.int32)
            return (jnp.where(core == 0, first, second) ^ r ^ z) * 2 + core

        pos = jnp.concatenate([chunks(c), chunks(1 - c)])
        pos = (pos[:, None] * rows + jnp.arange(rows, dtype=jnp.int32)[None, :]).reshape(-1)
        piece = R * rows // 2

        def each(f, pieces):
            return [f(v) for v in pieces]

        def join(pieces):
            return jnp.concatenate(pieces, axis=0)

        def cut4(v):
            return [v[k * piece : (k + 1) * piece] for k in range(4)]

        def total_tn(x, y):
            return mm_tn(join(x), join(y)).astype(BF)

        def plane_sum(x, w, product=mm_nt):
            return links.scatter_sum(lambda k: product(x[k], w))

        def sum_layers(g):
            return lax.psum_scatter(g, "z", scatter_dimension=0, tiled=True)

        def to_core(g):
            n = g.shape[0] // 2
            keep = lax.dynamic_slice_in_dim(g, c * n, n, 0)
            send = lax.dynamic_slice_in_dim(g, (1 - c) * n, n, 0)
            return jnp.concatenate([keep, links.core(send)], axis=1)

        def place(parts, index, cuts, shapes):
            here = jnp.stack([index, c]).astype(jnp.int32)
            return place_blocks(links, here, parts, cuts, shapes)

        def columns(start, span, outer, w, core_first, out):
            def spot(o, j, cc):
                return o * 2 * R * w + (cc * R + j if core_first else j * 2 + cc) * w

            return [
                (out, start + e * span + o * w, w, e, lambda j, cc, o=o: (0, spot(o, j, cc)))
                for o in range(outer)
                for e in range(2)
            ]

        x = x_low.astype(F32)
        a1, n1, i1 = layer_norm(x, gains[0], shifts[0])
        a1 = links.gather(a1)
        memory = links.to_plane(after(encoded[0], w_self))
        joined = each(lambda v: mm(v, w_self), a1)
        q1 = join([(v[:, :rank_cols] + pair_bias[0]).astype(BF) for v in joined])
        k1 = join([v[:, rank_cols : 2 * rank_cols].astype(BF) for v in joined])
        v1 = join([(v[:, 2 * rank_cols :] + pair_bias[1]).astype(BF) for v in joined])
        c1, l1 = attend(q1, k1, v1, pos, True)
        c1 = cut4(after(c1, memory))
        h1 = after(x + (plane_sum(c1, w_self_out, mm) + branch[0]), w_cross)
        a2, n2, i2 = layer_norm(h1, gains[1], shifts[1])
        seed_low = links.to_plane(after(cotangent[0], a2))
        seed = seed_low.astype(F32)
        a2, memory_all = links.gather(a2, memory)
        joined = each(lambda v: mm(v, w_cross_kv), memory_all)
        k2 = join([v[:, :rank_cols].astype(BF) for v in joined])
        v2 = join([(v[:, rank_cols:] + pair_bias[3]).astype(BF) for v in joined])
        q2 = join([(mm(v, w_cross_q) + pair_bias[2]).astype(BF) for v in a2])
        c2, l2 = attend(after(q2, seed_low), k2, v2, pos, False)
        c2 = cut4(after(c2, w_up, w_down))
        h2 = h1 + (plane_sum(c2, w_cross_out, mm) + branch[1])
        a3, n3, i3 = layer_norm(h2, gains[2], shifts[2])
        a3, seed_all = links.gather(a3, seed_low)

        def feed(v, s):
            pre = mm(v, w_up) + up_bias
            cdf = 0.5 * (1.0 + lax.erf(pre * (0.5 ** 0.5)))
            slope = cdf + pre * (jnp.exp(-0.5 * pre * pre) * (0.5 / jnp.pi) ** 0.5)
            return (pre * cdf).astype(BF), (slope * mm_nt(s, w_down)).astype(BF)

        fed = [feed(a3[k], seed_all[k]) for k in range(4)]
        act = [f[0] for f in fed]
        gz = [f[1] for f in fed]

        lifted, s3, t3 = norm_backward(plane_sum(gz, w_up), n3, i3, gains[2])
        act_all, seed_rows = join(act), join(seed_all)
        down_grad = [
            mm_tn(act_all, seed_rows[:, g * width : (g + 1) * width]).astype(BF).reshape(Z, sub, width)
            for g in range(groups)
        ]
        down_grad = jnp.stack(down_grad, axis=1).reshape(D, width)
        ffn_grad = jnp.concatenate([total_tn(a3, gz), down_grad], axis=1)
        d2 = seed + lifted
        ffn_grad = sum_layers(ffn_grad)
        g2 = d2.astype(BF)
        g2_all = links.gather(g2)
        e2 = join([mm_nt(v, w_cross_out).astype(BF) for v in g2_all])
        gq2, gk2, gv2 = attend_back(q2, k2, v2, e2, join(c2), l2, pos, False)
        output = (h2 + (plane_sum(act, after(w_down, g2_all[0]), mm) + branch[2])).astype(BF)
        cross_out_grad = total_tn(c2, g2_all)
        pair2 = jnp.concatenate([gk2, gv2], axis=1)
        cross_grad = jnp.concatenate(
            [mm_tn(join(a2), gq2).astype(BF), mm_tn(join(memory_all), pair2).astype(BF)], axis=1
        )
        lifted, s2, t2 = norm_backward(plane_sum(cut4(gq2), w_cross_q), n2, i2, gains[1])
        d1 = after(d2 + lifted, cross_grad, cross_out_grad, ffn_grad, output)
        g1 = d1.astype(BF)
        g1_all = links.gather(g1)
        e1 = join([mm_nt(v, w_self_out).astype(BF) for v in g1_all])
        gq1, gk1, gv1 = attend_back(q1, k1, v1, e1, join(c1), l1, pos, True)
        encoded_grad = plane_sum(cut4(after(pair2, g1_all[3])), w_cross_kv).astype(BF)

        output = links.from_plane(output)
        triple = after(jnp.concatenate([gq1, gk1, gv1], axis=1), encoded_grad, output)
        self_grad = mm_tn(join(a1), triple).astype(BF)
        self_out_grad = total_tn(c1, g1_all)
        out_grad = jnp.concatenate([cross_out_grad, self_out_grad], axis=0)
        far_chip = [jnp.where(c == 0, links.offset(p, 0), links.offset(p, 1)) for p in range(R)]
        out_grad = links.spread_chips(
            [lax.dynamic_slice_in_dim(out_grad, (r ^ f) * quarter, quarter, 1) for f in far_chip]
        )
        turned = [out_grad[links.reverse(p)] for p in range(R)]
        out_grad = ordered([jnp.where(c == 0, p, t) for p, t in zip(out_grad, turned)], r)
        out_grad = lax.optimization_barrier(jnp.concatenate(lax.optimization_barrier(out_grad), axis=0))
        triple = after(triple, self_grad)
        lifted, s1, t1 = norm_backward(plane_sum(cut4(triple), w_self), n1, i1, gains[0])
        hidden_grad = links.from_plane((d1 + lifted).astype(BF))
        down = ffn_grad[:, width:]
        cuts = columns(0, width, Z, sub, True, 0)
        ffn_pack = to_core(ffn_grad[:, :width])
        if sub == own:
            ffn_pack = jnp.concatenate([ffn_pack, down[:own], down[own:]], axis=1)
            cuts.append((1, 2 * width, D, 0, lambda j, cc: (j * sub, 0)))
        ffn_parts = links.gather_parts(after(ffn_pack, lifted))
        if sub == own:
            ffn_in_grad, ffn_out_grad = place(ffn_parts, r, cuts, [(own, FF), (R * sub, D)])
        else:
            (ffn_in_grad,) = place(ffn_parts, r, cuts, [(own, FF)])
            down = down.reshape(groups, sub, width).transpose(1, 0, 2).reshape(sub, D)
            cuts = [(0, 0, D, 0, lambda j, cc: (j * sub, 0))]
            (ffn_out_grad,) = place(links.gather_parts(down), r, cuts, [(R * sub, D)])
        encoded_grad = links.from_plane(after(encoded_grad, hidden_grad))

        span = 6 * rank_cols
        pack = sum_layers(jnp.concatenate([cross_grad, self_grad, out_grad], axis=1))
        pack = after(pack, hidden_grad, *ffn_parts)
        out_grad = pack[:, span:]
        pack = [to_core(pack[:, :span]), out_grad[:own], out_grad[own:]]
        parts = links.gather_parts(jnp.concatenate(pack, axis=1))
        parts = lax.optimization_barrier(tuple(parts) + (encoded_grad,))[:R]
        cross_both, self_qkv_grad = place(
            parts,
            r,
            columns(0, span, 3, rank_cols, False, 0)
            + columns(3 * rank_cols, span, 3, rank_cols, False, 1),
            [(own, 3 * D), (own, 3 * D)],
        )
        cross_q_grad = cross_both[:, :D]
        cross_kv_grad = cross_both[:, D:]
        cross_out_grad, self_out_grad = place(
            parts,
            r,
            [(i, 2 * span + i * quarter, quarter, 0, lambda j, cc: (0, j * quarter)) for i in range(2)],
            [(own, D), (own, D)],
        )

        def sum_small(v):
            k = v.shape[0]
            blocks = v.reshape(k, Z, 2, own).transpose(2, 1, 0, 3)
            away = lax.dynamic_index_in_dim(blocks, 1 - c, 0, False)
            near = lax.dynamic_index_in_dim(blocks, c, 0, False) + links.core(away)
            return links.sum_chips(links.scatter_layers(near, z))

        def spread(v):
            return lax.dynamic_update_slice(
                jnp.zeros((v.shape[0], D), F32), v, (zero, rank * rank_cols)
            )

        up_sums = sum(col_sum(v) for v in gz).reshape(Z, 1, 1, sub)
        up_sums = lax.dynamic_update_slice(jnp.zeros((Z, 2, R, sub), F32), up_sums, (zero, c, r, zero))
        up_sums = up_sums.reshape(2 * Z, up_rows, own).transpose(1, 0, 2).reshape(up_rows, D)
        sums = jnp.concatenate(
            [
                jnp.stack([s1, s2, s3, t1, t2, t3]),
                spread(jnp.stack([col_sum(gq1), col_sum(gv1), col_sum(gq2), col_sum(gv2)])),
                jnp.stack([col_sum(g1), col_sum(g2), col_sum(seed_low)]),
                up_sums,
            ],
            axis=0,
        )
        sums = sum_small(after(sums, hidden_grad, *ffn_parts))
        return (
            output[None],
            hidden_grad.astype(F32)[None],
            encoded_grad.astype(F32)[None],
            sums[0:3].T,
            sums[3:6].T,
            sums[6:10].T,
            sums[10:13].T,
            self_qkv_grad,
            self_out_grad,
            cross_q_grad,
            cross_kv_grad,
            cross_out_grad,
            ffn_in_grad,
            sums[13:].reshape(-1),
            ffn_out_grad,
        )

    return on_device


def solution(mesh):
    R = mesh.shape["replica"]
    Z = mesh.shape["shard"] // 2
    inner = Mesh(mesh.devices.reshape(R, Z, 2), AXES)
    rows = P("r", ("z", "c"), None)
    weight = P(("z", "c"), None)
    line = P(("z", "c"))
    return jax.shard_map(
        make(R, Z),
        mesh=inner,
        in_specs=(rows,) * 3 + (weight,) * 10 + (line, weight),
        out_specs=(rows,) * 3 + (weight,) * 10 + (line, weight),
        check_vma=False,
    )
```

```python
import jax
import jax.numpy as jnp
from jax import lax
from jax.experimental import pallas as pl
from jax.experimental.pallas import tpu as pltpu
from jax.sharding import Mesh
from jax.sharding import PartitionSpec as P

HEAD_DIM = 64
AXES = ("r", "z", "c")
BF = jnp.bfloat16
F32 = jnp.float32


def mm(a, b):
    return jnp.dot(a, b, preferred_element_type=F32)


def mm_tn(a, b):
    return lax.dot_general(a, b, (((0,), (0,)), ((), ())), preferred_element_type=F32)


def mm_nt(a, b):
    return lax.dot_general(a, b, (((1,), (1,)), ((), ())), preferred_element_type=F32)


def layer_norm(v, gain, shift):
    average = jnp.mean(v, axis=-1, keepdims=True)
    centred = v - average
    variance = jnp.mean(centred * centred, axis=-1, keepdims=True)
    inverse = lax.rsqrt(variance + 1e-05)
    normed = centred * inverse
    return (normed * gain + shift).astype(BF), normed, inverse


def norm_backward(grad, normed, inverse, gain):
    gain_grad = jnp.sum(grad * normed, axis=0)
    shift_grad = jnp.sum(grad, axis=0)
    scaled = grad * gain
    projected = (
        scaled
        - jnp.mean(scaled, axis=-1, keepdims=True)
        - normed * jnp.mean(scaled * normed, axis=-1, keepdims=True)
    )
    return inverse * projected, gain_grad, shift_grad


class Links:
    def __init__(self, planes_r, planes_z):
        self.R = planes_r
        self.Z = planes_z
        self.K = planes_r.bit_length() - 1
        self.M = planes_z.bit_length() - 1
        assert planes_r == 1 << self.K and planes_z == 1 << self.M

    def go(self, x, move):
        pairs = []
        for r in range(self.R):
            for z in range(self.Z):
                for c in range(2):
                    r2, z2, c2 = move(r, z, c)
                    pairs.append(((r * self.Z + z) * 2 + c, (r2 * self.Z + z2) * 2 + c2))
        return lax.ppermute(x, AXES, pairs)

    def to_plane(self, x):
        return self.go(x, lambda r, z, c: (z ^ r, r, c))

    def from_plane(self, x):
        return self.go(x, lambda r, z, c: (z, r ^ z, c))

    def core(self, x):
        return self.go(x, lambda r, z, c: (r, z, 1 - c))

    def bit(self, i, c):
        return i if c == 0 else self.K - 1 - i

    def step(self, x, i):
        return self.go(x, lambda r, z, c: (r ^ (1 << self.bit(i, c)), z, c))

    def same_step(self, x, i):
        return self.go(x, lambda r, z, c: (r ^ (1 << i), z, c))

    def layer_step(self, x, i):
        return self.go(x, lambda r, z, c: (r, z ^ (1 << i), c))

    def offset(self, p, c):
        return sum(1 << self.bit(i, c) for i in range(self.K) if p >> i & 1)

    def reverse(self, p):
        return sum(1 << (self.K - 1 - i) for i in range(self.K) if p >> i & 1)

    def gather(self, *xs):
        xs = list(xs)
        for i in range(self.K):
            n = xs[0].shape[0]
            got = self.step(jnp.concatenate(xs, axis=0) if len(xs) > 1 else xs[0], i)
            got = [got[k * n : (k + 1) * n] for k in range(len(xs))]
            if i < self.K - 1:
                xs = [jnp.concatenate([x, g], axis=0) for x, g in zip(xs, got)]
        far = [(self.core(x), self.core(g)) for x, g in zip(xs, got)]
        out = [(x, g) + f for x, g, f in zip(xs, got, far)]
        return out if len(out) > 1 else out[0]

    def scatter_sum(self, term):
        part = {}
        for k in (1, 0):
            away = self.core(term(2 + k).astype(BF))
            part[k] = term(k) + away.astype(F32)
        total = part[0] + self.step(part[1].astype(BF), self.K - 1).astype(F32)
        for i in reversed(range(self.K - 1)):
            n = total.shape[0] // 2
            total = total[:n] + self.step(total[n:].astype(BF), i).astype(F32)
        return total

    def spread_chips(self, blocks):
        held = [(p, b) for p, b in enumerate(blocks)]
        for i in range(self.K):
            away = [m for m, (left, _) in enumerate(held) if left >> i & 1]
            n = held[0][1].shape[0]
            got = self.step(jnp.concatenate([held[m][1] for m in away], axis=0), i)
            for k, m in enumerate(away):
                held[m] = (held[m][0] ^ 1 << i, got[k * n : (k + 1) * n])
        return [b for _, b in held]

    def gather_parts(self, x):
        parts = [x]
        for i in range(self.K):
            parts = parts + [self.step(p, i) for p in parts]
        return parts

    def sum_chips(self, x):
        for i in range(self.K):
            x = x + self.same_step(x, i)
        return x

    def scatter_layers(self, blocks, z):
        for i in reversed(range(self.M)):
            n = blocks.shape[0] // 2
            bit = (z >> i) & 1
            keep = lax.dynamic_slice_in_dim(blocks, bit * n, n, 0)
            send = lax.dynamic_slice_in_dim(blocks, (1 - bit) * n, n, 0)
            got = self.layer_step(send, i)
            blocks = (keep.astype(F32) + got.astype(F32)).astype(blocks.dtype)
        return blocks[0]


def attend(q, k, v, pos, causal):
    heads = q.shape[1] // HEAD_DIM
    outs, lses = [], []
    for h in range(heads):
        cut = slice(h * HEAD_DIM, (h + 1) * HEAD_DIM)
        s = mm_nt(q[:, cut], k[:, cut]) * HEAD_DIM ** (-0.5)
        if causal:
            s = jnp.where(pos[:, None] >= pos[None, :], s, -1e30)
        m = jnp.max(s, axis=-1, keepdims=True)
        p = jnp.exp(s - m)
        t = jnp.sum(p, axis=-1, keepdims=True)
        outs.append(mm((p / t).astype(BF), v[:, cut]).astype(BF))
        lses.append(m + jnp.log(t))
    return jnp.concatenate(outs, axis=1), lses


def attend_back(q, k, v, e, context, lses, pos, causal):
    heads = q.shape[1] // HEAD_DIM
    dqs, dks, dvs = [], [], []
    for h in range(heads):
        cut = slice(h * HEAD_DIM, (h + 1) * HEAD_DIM)
        s = mm_nt(q[:, cut], k[:, cut]) * HEAD_DIM ** (-0.5)
        if causal:
            s = jnp.where(pos[:, None] >= pos[None, :], s, -1e30)
        p = jnp.exp(s - lses[h])
        dp = mm_nt(e[:, cut], v[:, cut])
        inner = jnp.sum(e[:, cut].astype(F32) * context[:, cut].astype(F32), axis=-1, keepdims=True)
        ds = (p * (dp - inner)).astype(BF)
        dqs.append((mm(ds, k[:, cut]) * HEAD_DIM ** (-0.5)).astype(BF))
        dks.append((mm_tn(ds, q[:, cut]) * HEAD_DIM ** (-0.5)).astype(BF))
        dvs.append(mm_tn(p.astype(BF), e[:, cut]).astype(BF))
    return tuple(jnp.concatenate(g, axis=1) for g in (dqs, dks, dvs))


def after(x, *what):
    return lax.optimization_barrier((x,) + what)[0]


def col_sum(v):
    return jnp.sum(v.astype(F32), axis=0)


def ordered(parts, index):
    n = len(parts)
    outs = []
    for k in range(n):
        v = parts[k]
        for d in range(1, n):
            v = jnp.where(index == d, parts[k ^ d], v)
        outs.append(v)
    return outs


def pick_ffn(core, gathered, Z, own, sub, width, groups):
    half = groups // 2

    def kernel(core_ref, in_ref, up_ref, down_ref):
        core = core_ref[0]
        for s in range(2 * Z):
            up_ref[pl.ds(s * own, own)] = in_ref[core, pl.ds(s * 2 * own, own)]
        for z in range(Z):
            for g in range(groups):
                row = pl.multiple_of((z * 2 + core) * 2 * own + own + (g % half) * sub, 16)
                piece = in_ref[g // half, pl.ds(row, sub)]
                down_ref[pl.ds(z * sub, sub), pl.ds(g * width, width)] = piece

    D = gathered.shape[1] // 2
    vmem = pl.BlockSpec(memory_space=pltpu.VMEM)
    return pl.pallas_call(
        kernel,
        out_shape=[jax.ShapeDtypeStruct((D, width), BF), jax.ShapeDtypeStruct((width, D), BF)],
        in_specs=[pl.BlockSpec(memory_space=pltpu.SMEM), vmem],
        out_specs=[vmem, vmem],
        compiler_params=pltpu.CompilerParams(vmem_limit_bytes=24 << 20),
        cost_estimate=pl.CostEstimate(flops=0, transcendentals=0, bytes_accessed=8 << 20),
    )(core, gathered)


def place_blocks(links, here, parts, cuts, shapes):
    R = links.R
    aligned = all(w % 128 == 0 for _, _, w, _, _ in cuts)
    if not aligned:
        outs = [jnp.zeros(shape, F32) for shape in shapes]
        for p in range(R):
            for out, start, w, e, spot in cuts:
                chip = here[0] ^ jnp.where(here[1] == 0, links.offset(p, 0), links.offset(p, 1))
                at = tuple(jnp.int32(v) for v in spot(chip, here[1] ^ e))
                piece = parts[p][:, start : start + w].astype(F32)
                outs[out] = lax.dynamic_update_slice(outs[out], piece, at)
        return outs

    def kernel(here_ref, *refs):
        ins, outs = refs[:R], refs[R:]
        core = here_ref[1]
        for p in range(R):
            chip = here_ref[0] ^ jnp.where(core == 0, links.offset(p, 0), links.offset(p, 1))
            for out, start, w, e, spot in cuts:
                row, col = spot(chip, core ^ e)
                n = ins[p].shape[0]
                row = row if isinstance(row, int) else pl.multiple_of(row, n)
                col = col if isinstance(col, int) else pl.multiple_of(col, 128)
                piece = ins[p][:, start : start + w].astype(F32)
                outs[out][pl.ds(row, n), pl.ds(col, w)] = piece

    return pl.pallas_call(
        kernel,
        out_shape=[jax.ShapeDtypeStruct(shape, F32) for shape in shapes],
        in_specs=[pl.BlockSpec(memory_space=pltpu.SMEM)]
        + [pl.BlockSpec(memory_space=pltpu.VMEM)] * R,
        out_specs=[pl.BlockSpec(memory_space=pltpu.VMEM)] * len(shapes),
        compiler_params=pltpu.CompilerParams(vmem_limit_bytes=40 << 20),
        cost_estimate=pl.CostEstimate(flops=0, transcendentals=0, bytes_accessed=12 << 20),
    )(here, *parts)


def make(R, Z):
    links = Links(R, Z)

    def on_device(
        hidden, encoded, cotangent, norm_gain, norm_bias, attn_bias, out_bias,
        self_qkv, self_out, cross_q, cross_kv, cross_out, ffn_in, ffn_in_bias, ffn_out,
    ):
        r = lax.axis_index("r")
        z = lax.axis_index("z")
        c = lax.axis_index("c")
        rank = r * 2 + c
        rows = hidden.shape[1]
        D = hidden.shape[2]
        own = self_out.shape[0]
        rank_cols = D // (2 * R)
        FF = ffn_in.shape[1]
        sub = ffn_out.shape[0] // R
        up_rows = FF // D
        quarter = D // Z
        zero = jnp.int32(0)

        x_low = links.to_plane(hidden[0])

        def chip_columns(w, width):
            cut = lax.dynamic_index_in_dim(w.reshape(own, -1, R, 2, width), r, 2, False)
            return cut.transpose(2, 0, 1, 3).reshape(2, own, -1)

        def gather_layers(cut):
            full = lax.all_gather(cut, ("z", "c"), axis=1, tiled=True)
            return lax.dynamic_index_in_dim(full, c, 0, False)

        w_out = jnp.concatenate([self_out, cross_out], axis=0)
        w_out = lax.dynamic_slice_in_dim(w_out, (r ^ z) * quarter, quarter, 1)
        w_out = links.from_plane(w_out).reshape(2, own, quarter)
        cut_self = jnp.concatenate([chip_columns(self_qkv, rank_cols), w_out], axis=2)
        w_self = lax.all_gather(after(cut_self, x_low), ("z", "c"), axis=1, tiled=True)
        w_out = w_self[:, :, 3 * rank_cols :].reshape(2, Z, 2, own, quarter)
        w_out = lax.dynamic_index_in_dim(w_out, c, 2, False)
        w_self_out = jnp.concatenate([w_out[0, i] for i in range(Z)], axis=1)
        w_cross_out = jnp.concatenate([w_out[1, i] for i in range(Z)], axis=1)
        w_self = lax.dynamic_index_in_dim(w_self[:, :, : 3 * rank_cols], c, 0, False)
        cut_cross = chip_columns(jnp.concatenate([cross_q, cross_kv], axis=1), rank_cols)
        w_cross = gather_layers(after(cut_cross, x_low))
        w_cross_q = w_cross[:, :rank_cols]
        w_cross_kv = w_cross[:, rank_cols:]
        width = Z * sub
        groups = D // width
        cut_up = lax.dynamic_index_in_dim(ffn_in.reshape(own, Z, 2, R, sub), r, 3, False)
        cut_up = cut_up.transpose(2, 0, 1, 3).reshape(2, own, width)
        cut_down = lax.dynamic_slice_in_dim(ffn_out, r * sub, sub, 0)
        cut_down = jnp.concatenate(
            [cut_down[:, g * width : (g + 1) * width] for g in range(groups)], axis=0
        ).reshape(2, own, width)
        cut_ffn = after(jnp.concatenate([cut_up, cut_down], axis=1), x_low)
        w_ffn = lax.all_gather(cut_ffn, ("z", "c"), axis=1, tiled=True)
        w_up, w_down = pick_ffn(jnp.stack([c]).astype(jnp.int32), w_ffn, Z, own, sub, width, groups)

        vec = jnp.concatenate(
            [norm_gain.T, norm_bias.T, attn_bias.T, out_bias.T, ffn_in_bias.reshape(up_rows, own)],
            axis=0,
        )
        vec = after(vec, x_low)
        vec = jnp.concatenate(ordered([vec, links.core(vec)], c), axis=1)
        for i in range(links.M):
            vec = jnp.concatenate(ordered([vec, links.layer_step(vec, i)], (z >> i) & 1), axis=1)
        vec = vec.astype(F32)
        gains, shifts, branch = vec[0:3], vec[3:6], vec[10:13]
        pair_bias = lax.dynamic_slice_in_dim(vec[6:10], rank * rank_cols, rank_cols, 1)
        up_bias = vec[13:].reshape(up_rows, 2 * Z, own).transpose(1, 0, 2).reshape(Z, 2, R, sub)
        up_bias = lax.dynamic_index_in_dim(up_bias, c, 1, False)
        up_bias = lax.dynamic_index_in_dim(up_bias, r, 1, False).reshape(width)

        def chunks(core):
            first = jnp.array([links.offset(p, 0) for p in range(R)], jnp.int32)
            second = jnp.array([links.offset(p, 1) for p in range(R)], jnp.int32)
            return (jnp.where(core == 0, first, second) ^ r ^ z) * 2 + core

        pos = jnp.concatenate([chunks(c), chunks(1 - c)])
        pos = (pos[:, None] * rows + jnp.arange(rows, dtype=jnp.int32)[None, :]).reshape(-1)
        piece = R * rows // 2

        def each(f, pieces):
            return [f(v) for v in pieces]

        def join(pieces):
            return jnp.concatenate(pieces, axis=0)

        def cut4(v):
            return [v[k * piece : (k + 1) * piece] for k in range(4)]

        def total_tn(x, y):
            return mm_tn(join(x), join(y)).astype(BF)

        def plane_sum(x, w, product=mm_nt):
            return links.scatter_sum(lambda k: product(x[k], w))

        def sum_layers(g):
            return lax.psum_scatter(g, "z", scatter_dimension=0, tiled=True)

        def to_core(g):
            n = g.shape[0] // 2
            keep = lax.dynamic_slice_in_dim(g, c * n, n, 0)
            send = lax.dynamic_slice_in_dim(g, (1 - c) * n, n, 0)
            return jnp.concatenate([keep, links.core(send)], axis=1)

        def place(parts, index, cuts, shapes):
            here = jnp.stack([index, c]).astype(jnp.int32)
            return place_blocks(links, here, parts, cuts, shapes)

        def columns(start, span, outer, w, core_first, out):
            def spot(o, j, cc):
                return o * 2 * R * w + (cc * R + j if core_first else j * 2 + cc) * w

            return [
                (out, start + e * span + o * w, w, e, lambda j, cc, o=o: (0, spot(o, j, cc)))
                for o in range(outer)
                for e in range(2)
            ]

        x = x_low.astype(F32)
        a1, n1, i1 = layer_norm(x, gains[0], shifts[0])
        a1 = links.gather(a1)
        memory = links.to_plane(after(encoded[0], w_self))
        joined = each(lambda v: mm(v, w_self), a1)
        q1 = join([(v[:, :rank_cols] + pair_bias[0]).astype(BF) for v in joined])
        k1 = join([v[:, rank_cols : 2 * rank_cols].astype(BF) for v in joined])
        v1 = join([(v[:, 2 * rank_cols :] + pair_bias[1]).astype(BF) for v in joined])
        c1, l1 = attend(q1, k1, v1, pos, True)
        c1 = cut4(after(c1, memory))
        h1 = after(x + (plane_sum(c1, w_self_out, mm) + branch[0]), w_cross)
        a2, n2, i2 = layer_norm(h1, gains[1], shifts[1])
        seed_low = links.to_plane(after(cotangent[0], a2))
        seed = seed_low.astype(F32)
        a2, memory_all = links.gather(a2, memory)
        joined = each(lambda v: mm(v, w_cross_kv), memory_all)
        k2 = join([v[:, :rank_cols].astype(BF) for v in joined])
        v2 = join([(v[:, rank_cols:] + pair_bias[3]).astype(BF) for v in joined])
        q2 = join([(mm(v, w_cross_q) + pair_bias[2]).astype(BF) for v in a2])
        c2, l2 = attend(after(q2, seed_low), k2, v2, pos, False)
        c2 = cut4(after(c2, w_up, w_down))
        h2 = h1 + (plane_sum(c2, w_cross_out, mm) + branch[1])
        a3, n3, i3 = layer_norm(h2, gains[2], shifts[2])
        a3, seed_all = links.gather(a3, seed_low)

        def feed(v, s):
            pre = mm(v, w_up) + up_bias
            cdf = 0.5 * (1.0 + lax.erf(pre * (0.5 ** 0.5)))
            slope = cdf + pre * (jnp.exp(-0.5 * pre * pre) * (0.5 / jnp.pi) ** 0.5)
            return (pre * cdf).astype(BF), (slope * mm_nt(s, w_down)).astype(BF)

        fed = [feed(a3[k], seed_all[k]) for k in range(4)]
        act = [f[0] for f in fed]
        gz = [f[1] for f in fed]

        lifted, s3, t3 = norm_backward(plane_sum(gz, w_up), n3, i3, gains[2])
        act_all, seed_rows = join(act), join(seed_all)
        down_grad = [
            mm_tn(act_all, seed_rows[:, g * width : (g + 1) * width]).astype(BF).reshape(Z, sub, width)
            for g in range(groups)
        ]
        down_grad = jnp.stack(down_grad, axis=1).reshape(D, width)
        ffn_grad = jnp.concatenate([total_tn(a3, gz), down_grad], axis=1)
        d2 = seed + lifted
        ffn_grad = sum_layers(ffn_grad)
        g2 = d2.astype(BF)
        g2_all = links.gather(g2)
        e2 = join([mm_nt(v, w_cross_out).astype(BF) for v in g2_all])
        gq2, gk2, gv2 = attend_back(q2, k2, v2, e2, join(c2), l2, pos, False)
        output = (h2 + (plane_sum(act, after(w_down, g2_all[0]), mm) + branch[2])).astype(BF)
        cross_out_grad = total_tn(c2, g2_all)
        pair2 = jnp.concatenate([gk2, gv2], axis=1)
        cross_grad = jnp.concatenate(
            [mm_tn(join(a2), gq2).astype(BF), mm_tn(join(memory_all), pair2).astype(BF)], axis=1
        )
        lifted, s2, t2 = norm_backward(plane_sum(cut4(gq2), w_cross_q), n2, i2, gains[1])
        d1 = after(d2 + lifted, cross_grad, cross_out_grad, ffn_grad, output)
        g1 = d1.astype(BF)
        g1_all = links.gather(g1)
        e1 = join([mm_nt(v, w_self_out).astype(BF) for v in g1_all])
        gq1, gk1, gv1 = attend_back(q1, k1, v1, e1, join(c1), l1, pos, True)
        encoded_grad = plane_sum(cut4(after(pair2, g1_all[0])), w_cross_kv).astype(BF)

        output = links.from_plane(output)
        triple = after(jnp.concatenate([gq1, gk1, gv1], axis=1), encoded_grad, output)
        self_grad = mm_tn(join(a1), triple).astype(BF)
        self_out_grad = total_tn(c1, g1_all)
        out_grad = jnp.concatenate([cross_out_grad, self_out_grad], axis=0)
        far_chip = [jnp.where(c == 0, links.offset(p, 0), links.offset(p, 1)) for p in range(R)]
        out_grad = links.spread_chips(
            [lax.dynamic_slice_in_dim(out_grad, (r ^ f) * quarter, quarter, 1) for f in far_chip]
        )
        turned = [out_grad[links.reverse(p)] for p in range(R)]
        out_grad = ordered([jnp.where(c == 0, p, t) for p, t in zip(out_grad, turned)], r)
        out_grad = lax.optimization_barrier(jnp.concatenate(lax.optimization_barrier(out_grad), axis=0))
        triple = after(triple, self_grad)
        lifted, s1, t1 = norm_backward(plane_sum(cut4(triple), w_self), n1, i1, gains[0])
        hidden_grad = links.from_plane((d1 + lifted).astype(BF))
        down = ffn_grad[:, width:]
        cuts = columns(0, width, Z, sub, True, 0)
        ffn_pack = to_core(ffn_grad[:, :width])
        if sub == own:
            ffn_pack = jnp.concatenate([ffn_pack, down[:own], down[own:]], axis=1)
            cuts.append((1, 2 * width, D, 0, lambda j, cc: (j * sub, 0)))
        ffn_parts = links.gather_parts(after(ffn_pack, lifted))
        if sub == own:
            ffn_in_grad, ffn_out_grad = place(ffn_parts, r, cuts, [(own, FF), (R * sub, D)])
        else:
            (ffn_in_grad,) = place(ffn_parts, r, cuts, [(own, FF)])
            down = down.reshape(groups, sub, width).transpose(1, 0, 2).reshape(sub, D)
            cuts = [(0, 0, D, 0, lambda j, cc: (j * sub, 0))]
            (ffn_out_grad,) = place(links.gather_parts(down), r, cuts, [(R * sub, D)])
        encoded_grad = links.from_plane(after(encoded_grad, hidden_grad))

        span = 6 * rank_cols
        pack = sum_layers(jnp.concatenate([cross_grad, self_grad, out_grad], axis=1))
        pack = after(pack, hidden_grad, *ffn_parts)
        out_grad = pack[:, span:]
        pack = [to_core(pack[:, :span]), out_grad[:own], out_grad[own:]]
        parts = links.gather_parts(jnp.concatenate(pack, axis=1))
        parts = lax.optimization_barrier(tuple(parts) + (encoded_grad,))[:R]
        cross_both, self_qkv_grad = place(
            parts,
            r,
            columns(0, span, 3, rank_cols, False, 0)
            + columns(3 * rank_cols, span, 3, rank_cols, False, 1),
            [(own, 3 * D), (own, 3 * D)],
        )
        cross_q_grad = cross_both[:, :D]
        cross_kv_grad = cross_both[:, D:]
        cross_out_grad, self_out_grad = place(
            parts,
            r,
            [(i, 2 * span + i * quarter, quarter, 0, lambda j, cc: (0, j * quarter)) for i in range(2)],
            [(own, D), (own, D)],
        )

        def sum_small(v):
            k = v.shape[0]
            blocks = v.reshape(k, Z, 2, own).transpose(2, 1, 0, 3)
            away = lax.dynamic_index_in_dim(blocks, 1 - c, 0, False)
            near = lax.dynamic_index_in_dim(blocks, c, 0, False) + links.core(away)
            return links.sum_chips(links.scatter_layers(near, z))

        def spread(v):
            return lax.dynamic_update_slice(
                jnp.zeros((v.shape[0], D), F32), v, (zero, rank * rank_cols)
            )

        up_sums = sum(col_sum(v) for v in gz).reshape(Z, 1, 1, sub)
        up_sums = lax.dynamic_update_slice(jnp.zeros((Z, 2, R, sub), F32), up_sums, (zero, c, r, zero))
        up_sums = up_sums.reshape(2 * Z, up_rows, own).transpose(1, 0, 2).reshape(up_rows, D)
        sums = jnp.concatenate(
            [
                jnp.stack([s1, s2, s3, t1, t2, t3]),
                spread(jnp.stack([col_sum(gq1), col_sum(gv1), col_sum(gq2), col_sum(gv2)])),
                jnp.stack([col_sum(g1), col_sum(g2), col_sum(seed_low)]),
                up_sums,
            ],
            axis=0,
        )
        sums = sum_small(after(sums, hidden_grad, *ffn_parts))
        return (
            output[None],
            hidden_grad.astype(F32)[None],
            encoded_grad.astype(F32)[None],
            sums[0:3].T,
            sums[3:6].T,
            sums[6:10].T,
            sums[10:13].T,
            self_qkv_grad,
            self_out_grad,
            cross_q_grad,
            cross_kv_grad,
            cross_out_grad,
            ffn_in_grad,
            sums[13:].reshape(-1),
            ffn_out_grad,
        )

    return on_device


def solution(mesh):
    R = mesh.shape["replica"]
    Z = mesh.shape["shard"] // 2
    inner = Mesh(mesh.devices.reshape(R, Z, 2), AXES)
    rows = P("r", ("z", "c"), None)
    weight = P(("z", "c"), None)
    line = P(("z", "c"))
    return jax.shard_map(
        make(R, Z),
        mesh=inner,
        in_specs=(rows,) * 3 + (weight,) * 10 + (line, weight),
        out_specs=(rows,) * 3 + (weight,) * 10 + (line, weight),
        check_vma=False,
    )
```

```python
import jax
import jax.numpy as jnp
from jax import lax
from jax.experimental import pallas as pl
from jax.experimental.pallas import tpu as pltpu
from jax.sharding import Mesh
from jax.sharding import PartitionSpec as P

HEAD_DIM = 64
AXES = ("r", "z", "c")
BF = jnp.bfloat16
F32 = jnp.float32


def mm(a, b):
    return jnp.dot(a, b, preferred_element_type=F32)


def mm_tn(a, b):
    return lax.dot_general(a, b, (((0,), (0,)), ((), ())), preferred_element_type=F32)


def mm_nt(a, b):
    return lax.dot_general(a, b, (((1,), (1,)), ((), ())), preferred_element_type=F32)


def layer_norm(v, gain, shift):
    average = jnp.mean(v, axis=-1, keepdims=True)
    centred = v - average
    variance = jnp.mean(centred * centred, axis=-1, keepdims=True)
    inverse = lax.rsqrt(variance + 1e-05)
    normed = centred * inverse
    return (normed * gain + shift).astype(BF), normed, inverse


def norm_backward(grad, normed, inverse, gain):
    gain_grad = jnp.sum(grad * normed, axis=0)
    shift_grad = jnp.sum(grad, axis=0)
    scaled = grad * gain
    projected = (
        scaled
        - jnp.mean(scaled, axis=-1, keepdims=True)
        - normed * jnp.mean(scaled * normed, axis=-1, keepdims=True)
    )
    return inverse * projected, gain_grad, shift_grad


class Links:
    def __init__(self, planes_r, planes_z):
        self.R = planes_r
        self.Z = planes_z
        self.K = planes_r.bit_length() - 1
        self.M = planes_z.bit_length() - 1
        assert planes_r == 1 << self.K and planes_z == 1 << self.M

    def go(self, x, move):
        pairs = []
        for r in range(self.R):
            for z in range(self.Z):
                for c in range(2):
                    r2, z2, c2 = move(r, z, c)
                    pairs.append(((r * self.Z + z) * 2 + c, (r2 * self.Z + z2) * 2 + c2))
        return lax.ppermute(x, AXES, pairs)

    def to_plane(self, x):
        return self.go(x, lambda r, z, c: (z ^ r, r, c))

    def from_plane(self, x):
        return self.go(x, lambda r, z, c: (z, r ^ z, c))

    def core(self, x):
        return self.go(x, lambda r, z, c: (r, z, 1 - c))

    def bit(self, i, c):
        return i if c == 0 else self.K - 1 - i

    def step(self, x, i):
        return self.go(x, lambda r, z, c: (r ^ (1 << self.bit(i, c)), z, c))

    def same_step(self, x, i):
        return self.go(x, lambda r, z, c: (r ^ (1 << i), z, c))

    def layer_step(self, x, i):
        return self.go(x, lambda r, z, c: (r, z ^ (1 << i), c))

    def offset(self, p, c):
        return sum(1 << self.bit(i, c) for i in range(self.K) if p >> i & 1)

    def reverse(self, p):
        return sum(1 << (self.K - 1 - i) for i in range(self.K) if p >> i & 1)

    def gather(self, *xs):
        xs = list(xs)
        for i in range(self.K):
            n = xs[0].shape[0]
            got = self.step(jnp.concatenate(xs, axis=0) if len(xs) > 1 else xs[0], i)
            got = [got[k * n : (k + 1) * n] for k in range(len(xs))]
            if i < self.K - 1:
                xs = [jnp.concatenate([x, g], axis=0) for x, g in zip(xs, got)]
        far = [(self.core(x), self.core(g)) for x, g in zip(xs, got)]
        out = [(x, g) + f for x, g, f in zip(xs, got, far)]
        return out if len(out) > 1 else out[0]

    def scatter_sum(self, term):
        part = {}
        for k in (1, 0):
            away = self.core(term(2 + k).astype(BF))
            part[k] = term(k) + away.astype(F32)
        total = part[0] + self.step(part[1].astype(BF), self.K - 1).astype(F32)
        for i in reversed(range(self.K - 1)):
            n = total.shape[0] // 2
            total = total[:n] + self.step(total[n:].astype(BF), i).astype(F32)
        return total

    def spread_chips(self, blocks):
        held = [(p, b) for p, b in enumerate(blocks)]
        for i in range(self.K):
            away = [m for m, (left, _) in enumerate(held) if left >> i & 1]
            n = held[0][1].shape[0]
            got = self.step(jnp.concatenate([held[m][1] for m in away], axis=0), i)
            for k, m in enumerate(away):
                held[m] = (held[m][0] ^ 1 << i, got[k * n : (k + 1) * n])
        return [b for _, b in held]

    def gather_parts(self, x):
        parts = [x]
        for i in range(self.K):
            parts = parts + [self.step(p, i) for p in parts]
        return parts

    def sum_chips(self, x):
        for i in range(self.K):
            x = x + self.same_step(x, i)
        return x

    def scatter_layers(self, blocks, z):
        for i in reversed(range(self.M)):
            n = blocks.shape[0] // 2
            bit = (z >> i) & 1
            keep = lax.dynamic_slice_in_dim(blocks, bit * n, n, 0)
            send = lax.dynamic_slice_in_dim(blocks, (1 - bit) * n, n, 0)
            got = self.layer_step(send, i)
            blocks = (keep.astype(F32) + got.astype(F32)).astype(blocks.dtype)
        return blocks[0]


def attend(q, k, v, pos, causal):
    heads = q.shape[1] // HEAD_DIM
    outs, lses = [], []
    for h in range(heads):
        cut = slice(h * HEAD_DIM, (h + 1) * HEAD_DIM)
        s = mm_nt(q[:, cut] * BF(HEAD_DIM ** (-0.5)), k[:, cut])
        if causal:
            s = jnp.where(pos[:, None] >= pos[None, :], s, -1e30)
        m = jnp.max(s, axis=-1, keepdims=True)
        p = jnp.exp(s - m)
        t = jnp.sum(p, axis=-1, keepdims=True)
        outs.append(mm((p * (1.0 / t)).astype(BF), v[:, cut]).astype(BF))
        lses.append(m + jnp.log(t))
    return jnp.concatenate(outs, axis=1), lses


def attend_back(q, k, v, e, context, lses, pos, causal):
    heads = q.shape[1] // HEAD_DIM
    dqs, dks, dvs = [], [], []
    for h in range(heads):
        cut = slice(h * HEAD_DIM, (h + 1) * HEAD_DIM)
        s = mm_nt(q[:, cut] * BF(HEAD_DIM ** (-0.5)), k[:, cut])
        if causal:
            s = jnp.where(pos[:, None] >= pos[None, :], s, -1e30)
        p = jnp.exp(s - lses[h])
        dp = mm_nt(e[:, cut], v[:, cut])
        inner = jnp.sum(e[:, cut].astype(F32) * context[:, cut].astype(F32), axis=-1, keepdims=True)
        ds = (p * (dp - inner)).astype(BF)
        dqs.append((mm(ds, k[:, cut]) * HEAD_DIM ** (-0.5)).astype(BF))
        dks.append((mm_tn(ds, q[:, cut]) * HEAD_DIM ** (-0.5)).astype(BF))
        dvs.append(mm_tn(p.astype(BF), e[:, cut]).astype(BF))
    return tuple(jnp.concatenate(g, axis=1) for g in (dqs, dks, dvs))


def after(x, *what):
    return lax.optimization_barrier((x,) + what)[0]


def col_sum(v):
    return jnp.sum(v.astype(F32), axis=0)


def ordered(parts, index):
    n = len(parts)
    outs = []
    for k in range(n):
        v = parts[k]
        for d in range(1, n):
            v = jnp.where(index == d, parts[k ^ d], v)
        outs.append(v)
    return outs


def pick_ffn(core, gathered, Z, own, sub, width, groups):
    half = groups // 2

    def kernel(core_ref, in_ref, up_ref, down_ref):
        core = core_ref[0]
        for s in range(2 * Z):
            up_ref[pl.ds(s * own, own)] = in_ref[core, pl.ds(s * 2 * own, own)]
        for z in range(Z):
            for g in range(groups):
                row = pl.multiple_of((z * 2 + core) * 2 * own + own + (g % half) * sub, 16)
                piece = in_ref[g // half, pl.ds(row, sub)]
                down_ref[pl.ds(z * sub, sub), pl.ds(g * width, width)] = piece

    D = gathered.shape[1] // 2
    vmem = pl.BlockSpec(memory_space=pltpu.VMEM)
    return pl.pallas_call(
        kernel,
        out_shape=[jax.ShapeDtypeStruct((D, width), BF), jax.ShapeDtypeStruct((width, D), BF)],
        in_specs=[pl.BlockSpec(memory_space=pltpu.SMEM), vmem],
        out_specs=[vmem, vmem],
        compiler_params=pltpu.CompilerParams(vmem_limit_bytes=24 << 20),
        cost_estimate=pl.CostEstimate(flops=0, transcendentals=0, bytes_accessed=8 << 20),
    )(core, gathered)


def place_blocks(links, here, parts, cuts, shapes):
    R = links.R
    aligned = all(w % 128 == 0 for _, _, w, _, _ in cuts)
    if not aligned:
        outs = [jnp.zeros(shape, F32) for shape in shapes]
        for p in range(R):
            for out, start, w, e, spot in cuts:
                chip = here[0] ^ jnp.where(here[1] == 0, links.offset(p, 0), links.offset(p, 1))
                at = tuple(jnp.int32(v) for v in spot(chip, here[1] ^ e))
                piece = parts[p][:, start : start + w].astype(F32)
                outs[out] = lax.dynamic_update_slice(outs[out], piece, at)
        return outs

    def kernel(here_ref, *refs):
        ins, outs = refs[:R], refs[R:]
        core = here_ref[1]
        for p in range(R):
            chip = here_ref[0] ^ jnp.where(core == 0, links.offset(p, 0), links.offset(p, 1))
            for out, start, w, e, spot in cuts:
                row, col = spot(chip, core ^ e)
                n = ins[p].shape[0]
                row = row if isinstance(row, int) else pl.multiple_of(row, n)
                col = col if isinstance(col, int) else pl.multiple_of(col, 128)
                piece = ins[p][:, start : start + w].astype(F32)
                outs[out][pl.ds(row, n), pl.ds(col, w)] = piece

    return pl.pallas_call(
        kernel,
        out_shape=[jax.ShapeDtypeStruct(shape, F32) for shape in shapes],
        in_specs=[pl.BlockSpec(memory_space=pltpu.SMEM)]
        + [pl.BlockSpec(memory_space=pltpu.VMEM)] * R,
        out_specs=[pl.BlockSpec(memory_space=pltpu.VMEM)] * len(shapes),
        compiler_params=pltpu.CompilerParams(vmem_limit_bytes=40 << 20),
        cost_estimate=pl.CostEstimate(flops=0, transcendentals=0, bytes_accessed=12 << 20),
    )(here, *parts)


def make(R, Z):
    links = Links(R, Z)

    def on_device(
        hidden, encoded, cotangent, norm_gain, norm_bias, attn_bias, out_bias,
        self_qkv, self_out, cross_q, cross_kv, cross_out, ffn_in, ffn_in_bias, ffn_out,
    ):
        r = lax.axis_index("r")
        z = lax.axis_index("z")
        c = lax.axis_index("c")
        rank = r * 2 + c
        rows = hidden.shape[1]
        D = hidden.shape[2]
        own = self_out.shape[0]
        rank_cols = D // (2 * R)
        FF = ffn_in.shape[1]
        sub = ffn_out.shape[0] // R
        up_rows = FF // D
        quarter = D // Z
        zero = jnp.int32(0)

        x_low = links.to_plane(hidden[0])

        def chip_columns(w, width):
            cut = lax.dynamic_index_in_dim(w.reshape(own, -1, R, 2, width), r, 2, False)
            return cut.transpose(2, 0, 1, 3).reshape(2, own, -1)

        def gather_layers(cut):
            full = lax.all_gather(cut, ("z", "c"), axis=1, tiled=True)
            return lax.dynamic_index_in_dim(full, c, 0, False)

        w_out = jnp.concatenate([self_out, cross_out], axis=0)
        w_out = lax.dynamic_slice_in_dim(w_out, (r ^ z) * quarter, quarter, 1)
        w_out = links.from_plane(w_out).reshape(2, own, quarter)
        cut_self = jnp.concatenate([chip_columns(self_qkv, rank_cols), w_out], axis=2)
        w_self = lax.all_gather(after(cut_self, x_low), ("z", "c"), axis=1, tiled=True)
        w_out = w_self[:, :, 3 * rank_cols :].reshape(2, Z, 2, own, quarter)
        w_out = lax.dynamic_index_in_dim(w_out, c, 2, False)
        w_self_out = jnp.concatenate([w_out[0, i] for i in range(Z)], axis=1)
        w_cross_out = jnp.concatenate([w_out[1, i] for i in range(Z)], axis=1)
        w_self = lax.dynamic_index_in_dim(w_self[:, :, : 3 * rank_cols], c, 0, False)
        cut_cross = chip_columns(jnp.concatenate([cross_q, cross_kv], axis=1), rank_cols)
        w_cross = gather_layers(after(cut_cross, x_low))
        w_cross_q = w_cross[:, :rank_cols]
        w_cross_kv = w_cross[:, rank_cols:]
        width = Z * sub
        groups = D // width
        cut_up = lax.dynamic_index_in_dim(ffn_in.reshape(own, Z, 2, R, sub), r, 3, False)
        cut_up = cut_up.transpose(2, 0, 1, 3).reshape(2, own, width)
        cut_down = lax.dynamic_slice_in_dim(ffn_out, r * sub, sub, 0)
        cut_down = jnp.concatenate(
            [cut_down[:, g * width : (g + 1) * width] for g in range(groups)], axis=0
        ).reshape(2, own, width)
        cut_ffn = after(jnp.concatenate([cut_up, cut_down], axis=1), x_low)
        w_ffn = lax.all_gather(cut_ffn, ("z", "c"), axis=1, tiled=True)
        w_up, w_down = pick_ffn(jnp.stack([c]).astype(jnp.int32), w_ffn, Z, own, sub, width, groups)

        vec = jnp.concatenate(
            [norm_gain.T, norm_bias.T, attn_bias.T, out_bias.T, ffn_in_bias.reshape(up_rows, own)],
            axis=0,
        )
        vec = after(vec, x_low)
        vec = jnp.concatenate(ordered([vec, links.core(vec)], c), axis=1)
        for i in range(links.M):
            vec = jnp.concatenate(ordered([vec, links.layer_step(vec, i)], (z >> i) & 1), axis=1)
        vec = vec.astype(F32)
        gains, shifts, branch = vec[0:3], vec[3:6], vec[10:13]
        pair_bias = lax.dynamic_slice_in_dim(vec[6:10], rank * rank_cols, rank_cols, 1)
        up_bias = vec[13:].reshape(up_rows, 2 * Z, own).transpose(1, 0, 2).reshape(Z, 2, R, sub)
        up_bias = lax.dynamic_index_in_dim(up_bias, c, 1, False)
        up_bias = lax.dynamic_index_in_dim(up_bias, r, 1, False).reshape(width)

        def chunks(core):
            first = jnp.array([links.offset(p, 0) for p in range(R)], jnp.int32)
            second = jnp.array([links.offset(p, 1) for p in range(R)], jnp.int32)
            return (jnp.where(core == 0, first, second) ^ r ^ z) * 2 + core

        pos = jnp.concatenate([chunks(c), chunks(1 - c)])
        pos = (pos[:, None] * rows + jnp.arange(rows, dtype=jnp.int32)[None, :]).reshape(-1)
        piece = R * rows // 2

        def each(f, pieces):
            return [f(v) for v in pieces]

        def join(pieces):
            return jnp.concatenate(pieces, axis=0)

        def cut4(v):
            return [v[k * piece : (k + 1) * piece] for k in range(4)]

        def total_tn(x, y):
            return mm_tn(join(x), join(y)).astype(BF)

        def plane_sum(x, w, product=mm_nt):
            return links.scatter_sum(lambda k: product(x[k], w))

        def sum_layers(g):
            return lax.psum_scatter(g, "z", scatter_dimension=0, tiled=True)

        def to_core(g):
            n = g.shape[0] // 2
            keep = lax.dynamic_slice_in_dim(g, c * n, n, 0)
            send = lax.dynamic_slice_in_dim(g, (1 - c) * n, n, 0)
            return jnp.concatenate([keep, links.core(send)], axis=1)

        def place(parts, index, cuts, shapes):
            here = jnp.stack([index, c]).astype(jnp.int32)
            return place_blocks(links, here, parts, cuts, shapes)

        def columns(start, span, outer, w, core_first, out):
            def spot(o, j, cc):
                return o * 2 * R * w + (cc * R + j if core_first else j * 2 + cc) * w

            return [
                (out, start + e * span + o * w, w, e, lambda j, cc, o=o: (0, spot(o, j, cc)))
                for o in range(outer)
                for e in range(2)
            ]

        x = x_low.astype(F32)
        a1, n1, i1 = layer_norm(x, gains[0], shifts[0])
        a1 = links.gather(a1)
        memory = links.to_plane(after(encoded[0], w_self))
        joined = each(lambda v: mm(v, w_self), a1)
        q1 = join([(v[:, :rank_cols] + pair_bias[0]).astype(BF) for v in joined])
        k1 = join([v[:, rank_cols : 2 * rank_cols].astype(BF) for v in joined])
        v1 = join([(v[:, 2 * rank_cols :] + pair_bias[1]).astype(BF) for v in joined])
        c1, l1 = attend(q1, k1, v1, pos, True)
        c1 = cut4(after(c1, memory))
        h1 = after(x + (plane_sum(c1, w_self_out, mm) + branch[0]), w_cross)
        a2, n2, i2 = layer_norm(h1, gains[1], shifts[1])
        seed_low = links.to_plane(after(cotangent[0], a2))
        seed = seed_low.astype(F32)
        a2, memory_all = links.gather(a2, memory)
        joined = each(lambda v: mm(v, w_cross_kv), memory_all)
        k2 = join([v[:, :rank_cols].astype(BF) for v in joined])
        v2 = join([(v[:, rank_cols:] + pair_bias[3]).astype(BF) for v in joined])
        q2 = join([(mm(v, w_cross_q) + pair_bias[2]).astype(BF) for v in a2])
        c2, l2 = attend(after(q2, seed_low), k2, v2, pos, False)
        c2 = cut4(after(c2, w_up, w_down))
        h2 = h1 + (plane_sum(c2, w_cross_out, mm) + branch[1])
        a3, n3, i3 = layer_norm(h2, gains[2], shifts[2])
        a3, seed_all = links.gather(a3, seed_low)

        def feed(v, s):
            pre = mm(v, w_up) + up_bias
            cdf = 0.5 * (1.0 + lax.erf(pre * (0.5 ** 0.5)))
            slope = cdf + pre * (jnp.exp(-0.5 * pre * pre) * (0.5 / jnp.pi) ** 0.5)
            return (pre * cdf).astype(BF), (slope * mm_nt(s, w_down)).astype(BF)

        fed = [feed(a3[k], seed_all[k]) for k in range(4)]
        act = [f[0] for f in fed]
        gz = [f[1] for f in fed]

        lifted, s3, t3 = norm_backward(plane_sum(gz, w_up), n3, i3, gains[2])
        act_all, seed_rows = join(act), join(seed_all)
        down_grad = [
            mm_tn(act_all, seed_rows[:, g * width : (g + 1) * width]).astype(BF).reshape(Z, sub, width)
            for g in range(groups)
        ]
        down_grad = jnp.stack(down_grad, axis=1).reshape(D, width)
        ffn_grad = jnp.concatenate([total_tn(a3, gz), down_grad], axis=1)
        d2 = seed + lifted
        ffn_grad = sum_layers(ffn_grad)
        g2 = d2.astype(BF)
        g2_all = links.gather(g2)
        e2 = join([mm_nt(v, w_cross_out).astype(BF) for v in g2_all])
        gq2, gk2, gv2 = attend_back(q2, k2, v2, e2, join(c2), l2, pos, False)
        output = (h2 + (plane_sum(act, after(w_down, g2_all[0]), mm) + branch[2])).astype(BF)
        cross_out_grad = total_tn(c2, g2_all)
        pair2 = jnp.concatenate([gk2, gv2], axis=1)
        cross_grad = jnp.concatenate(
            [mm_tn(join(a2), gq2).astype(BF), mm_tn(join(memory_all), pair2).astype(BF)], axis=1
        )
        lifted, s2, t2 = norm_backward(plane_sum(cut4(gq2), w_cross_q), n2, i2, gains[1])
        d1 = after(d2 + lifted, cross_grad, cross_out_grad, ffn_grad, output)
        g1 = d1.astype(BF)
        g1_all = links.gather(g1)
        e1 = join([mm_nt(v, w_self_out).astype(BF) for v in g1_all])
        gq1, gk1, gv1 = attend_back(q1, k1, v1, e1, join(c1), l1, pos, True)
        encoded_grad = plane_sum(cut4(after(pair2, g1_all[0])), w_cross_kv).astype(BF)

        output = links.from_plane(output)
        triple = after(jnp.concatenate([gq1, gk1, gv1], axis=1), encoded_grad, output)
        self_grad = mm_tn(join(a1), triple).astype(BF)
        self_out_grad = total_tn(c1, g1_all)
        out_grad = jnp.concatenate([cross_out_grad, self_out_grad], axis=0)
        far_chip = [jnp.where(c == 0, links.offset(p, 0), links.offset(p, 1)) for p in range(R)]
        out_grad = links.spread_chips(
            [lax.dynamic_slice_in_dim(out_grad, (r ^ f) * quarter, quarter, 1) for f in far_chip]
        )
        turned = [out_grad[links.reverse(p)] for p in range(R)]
        out_grad = ordered([jnp.where(c == 0, p, t) for p, t in zip(out_grad, turned)], r)
        out_grad = lax.optimization_barrier(jnp.concatenate(lax.optimization_barrier(out_grad), axis=0))
        triple = after(triple, self_grad)
        lifted, s1, t1 = norm_backward(plane_sum(cut4(triple), w_self), n1, i1, gains[0])
        hidden_grad = links.from_plane((d1 + lifted).astype(BF))
        down = ffn_grad[:, width:]
        cuts = columns(0, width, Z, sub, True, 0)
        ffn_pack = to_core(ffn_grad[:, :width])
        if sub == own:
            ffn_pack = jnp.concatenate([ffn_pack, down[:own], down[own:]], axis=1)
            cuts.append((1, 2 * width, D, 0, lambda j, cc: (j * sub, 0)))
        ffn_parts = links.gather_parts(after(ffn_pack, lifted))
        if sub == own:
            ffn_in_grad, ffn_out_grad = place(ffn_parts, r, cuts, [(own, FF), (R * sub, D)])
        else:
            (ffn_in_grad,) = place(ffn_parts, r, cuts, [(own, FF)])
            down = down.reshape(groups, sub, width).transpose(1, 0, 2).reshape(sub, D)
            cuts = [(0, 0, D, 0, lambda j, cc: (j * sub, 0))]
            (ffn_out_grad,) = place(links.gather_parts(down), r, cuts, [(R * sub, D)])
        encoded_grad = links.from_plane(after(encoded_grad, hidden_grad))

        span = 6 * rank_cols
        pack = sum_layers(jnp.concatenate([cross_grad, self_grad, out_grad], axis=1))
        pack = after(pack, hidden_grad, *ffn_parts)
        out_grad = pack[:, span:]
        pack = [to_core(pack[:, :span]), out_grad[:own], out_grad[own:]]
        parts = links.gather_parts(jnp.concatenate(pack, axis=1))
        parts = lax.optimization_barrier(tuple(parts) + (encoded_grad,))[:R]
        cross_both, self_qkv_grad = place(
            parts,
            r,
            columns(0, span, 3, rank_cols, False, 0)
            + columns(3 * rank_cols, span, 3, rank_cols, False, 1),
            [(own, 3 * D), (own, 3 * D)],
        )
        cross_q_grad = cross_both[:, :D]
        cross_kv_grad = cross_both[:, D:]
        cross_out_grad, self_out_grad = place(
            parts,
            r,
            [(i, 2 * span + i * quarter, quarter, 0, lambda j, cc: (0, j * quarter)) for i in range(2)],
            [(own, D), (own, D)],
        )

        def sum_small(v):
            k = v.shape[0]
            blocks = v.reshape(k, Z, 2, own).transpose(2, 1, 0, 3)
            away = lax.dynamic_index_in_dim(blocks, 1 - c, 0, False)
            near = lax.dynamic_index_in_dim(blocks, c, 0, False) + links.core(away)
            return links.sum_chips(links.scatter_layers(near, z))

        def spread(v):
            return lax.dynamic_update_slice(
                jnp.zeros((v.shape[0], D), F32), v, (zero, rank * rank_cols)
            )

        up_sums = sum(col_sum(v) for v in gz).reshape(Z, 1, 1, sub)
        up_sums = lax.dynamic_update_slice(jnp.zeros((Z, 2, R, sub), F32), up_sums, (zero, c, r, zero))
        up_sums = up_sums.reshape(2 * Z, up_rows, own).transpose(1, 0, 2).reshape(up_rows, D)
        sums = jnp.concatenate(
            [
                jnp.stack([s1, s2, s3, t1, t2, t3]),
                spread(jnp.stack([col_sum(gq1), col_sum(gv1), col_sum(gq2), col_sum(gv2)])),
                jnp.stack([col_sum(g1), col_sum(g2), col_sum(seed_low)]),
                up_sums,
            ],
            axis=0,
        )
        sums = sum_small(after(sums, hidden_grad, *ffn_parts))
        return (
            output[None],
            hidden_grad.astype(F32)[None],
            encoded_grad.astype(F32)[None],
            sums[0:3].T,
            sums[3:6].T,
            sums[6:10].T,
            sums[10:13].T,
            self_qkv_grad,
            self_out_grad,
            cross_q_grad,
            cross_kv_grad,
            cross_out_grad,
            ffn_in_grad,
            sums[13:].reshape(-1),
            ffn_out_grad,
        )

    return on_device


def solution(mesh):
    R = mesh.shape["replica"]
    Z = mesh.shape["shard"] // 2
    inner = Mesh(mesh.devices.reshape(R, Z, 2), AXES)
    rows = P("r", ("z", "c"), None)
    weight = P(("z", "c"), None)
    line = P(("z", "c"))
    return jax.shard_map(
        make(R, Z),
        mesh=inner,
        in_specs=(rows,) * 3 + (weight,) * 10 + (line, weight),
        out_specs=(rows,) * 3 + (weight,) * 10 + (line, weight),
        check_vma=False,
    )
```
